32 devices in a mesh: rep: 2 (over x), fsdp: 4 (over z), tp: 4 (over y, core).
Axes of the slice: x: 2, y: 2, z: 4, core: 2. Of those that a mesh axis runs over, the one named last changes fastest.
Arguments:
- tokens: bfloat16 [4096, 8192], P(('rep', 'fsdp')), may hold values from -16 to 16, as said below
- doc_lengths: int32 [8, 8], P(('rep', 'fsdp')), may hold values from 1 to 192, 512 in all within a row
- w_query: bfloat16 [8192, 4096], P(('rep', 'fsdp'), 'tp'), as said below
- w_key: bfloat16 [8192, 512], P(('rep', 'fsdp'), 'tp'), as said below
- w_value: bfloat16 [8192, 512], P(('rep', 'fsdp'), 'tp'), may hold values from -0.0625 to 0.0625
- u_query: float32 [4096], P('tp'), may hold values from -6 to 6
- u_key: float32 [512], P('tp'), may hold values from -6 to 6
- u_value: float32 [512], P('tp'), may hold values from -6 to 6
- gammas: float32 [3], replicated, may hold values from 0.5 to 2
Outputs:
- context: bfloat16 [4096, 4096], P(('rep', 'fsdp'), 'tp')
- u_query_new: float32 [4096], P('tp')
- u_key_new: float32 [512], P('tp')
- u_value_new: float32 [512], P('tp')
- sigmas: float32 [3], replicated
The draws below stay inside these ranges and needn't reach their ends.
Inputs may be any that keep to these rules, and one draw needn't show every extreme that they name: `tokens`: activations of order one. `w_query`: entries of order one over the square root of 8192. `w_key`: entries of order one over the square root of 8192.
All inputs are finite; a program needn't handle non-finite values.
Results may differ from the reference program's by a relative error of at most 0.0075.
Values may be sent and summed in bfloat16 or wider, within the bound.
No kernel may reach another device: no remote copies, remote signals or barrier semaphores. Data moves between devices by JAX's collectives and lax.ppermute only.
A program may use at most 128 MiB of HBM per device.

```python
import math
import jax
import jax.numpy as jnp
import numpy as np
from jax import lax

D = 8192
HEADS = 32
KV_HEADS = 4
HD = 128
TOK_DEV = 512
DOCS = 8
DOC_MOST = 192
SEQS = 8
TOKENS = 4096
QW = 4096
KW = 512


def weight_pair(key):
    base_key = jax.random.fold_in(key, 11)
    first_key, second_key = jax.random.split(base_key, 2)
    query_part = jnp.clip(jax.random.normal(first_key, (D, HEADS * HD), jnp.float32), -6.0, 6.0) * D ** (-0.5)
    key_part = jnp.clip(jax.random.normal(second_key, (D, KV_HEADS * HD), jnp.float32), -6.0, 6.0) * D ** (-0.5)
    return (query_part, key_part)


def draw_w_query(key, part):
    return weight_pair(key)[0].astype(jnp.bfloat16)


def draw_w_key(key, part):
    return weight_pair(key)[1].astype(jnp.bfloat16)


def draw_tokens(key, part):
    first_key = jax.random.fold_in(jax.random.fold_in(key, 5), 0)
    result = jnp.clip(jax.random.normal(first_key, (TOKENS, D), jnp.float32), -6.0, 6.0)
    return result.astype(jnp.bfloat16)


def levels(rng, dims, shards, smallest, high):
    def one(dim, parts):
        steps = jax.random.uniform(jax.random.fold_in(jax.random.fold_in(rng, 6), dim), (parts,), jnp.float32, smallest / len(shards), high / len(shards))
        return jnp.repeat(jnp.exp(steps), dims[dim] // parts).reshape((-1,) + (1,) * (len(dims) - dim - 1))

    factor_of = one(*shards[0])
    for cut in shards[1:]:
        factor_of = factor_of * one(*cut)
    return factor_of


def length_profile(number_of, total, limit, lean):
    portions = [(1 << 20) // math.isqrt(rank ** lean) + 1 for rank in range(2, number_of + 1)]
    rest, counts = total - limit - (number_of - 1), [1] * (number_of - 1)
    while rest > 0:
        free = [i for i in range(number_of - 1) if counts[i] < limit]
        mass, budget = sum([portions[i] for i in free]), rest
        for i in free:
            more = min(limit - counts[i], max(1, budget * portions[i] // mass), rest)
            counts[i] = counts[i] + more
            rest = rest - more
    return np.array([limit] + counts)


def ragged_sizes(rng, amount, total, bound, skew):
    if amount == 2:
        one = jax.random.randint(rng, (), max(1, total - bound), min(bound, total - 1) + 1)
        return jnp.stack([one, total - one])
    sizes = jnp.asarray(length_profile(amount, total, bound, skew), jnp.int32)
    twos = (amount - 1) // 2
    donor, sink = sizes[1:1 + 2 * twos:2], sizes[2:2 + 2 * twos:2]
    margin = jnp.minimum(donor - 1, bound - sink)
    shifted = jax.random.randint(jax.random.fold_in(rng, 1), (twos,), 0, 1 << 20) % (margin + 1)
    sizes = sizes.at[1:1 + 2 * twos:2].set(donor - shifted).at[2:2 + 2 * twos:2].set(sink + shifted)
    return sizes[jax.random.permutation(jax.random.fold_in(rng, 2), amount)]


def noise(key, dims, width, bound, pieces=(), held_as=jnp.bfloat16):
    factor_of = levels(key, dims, pieces, -0.22, 0.18) if pieces else 1.0
    array = jax.random.normal(key, dims, jnp.float32) * width * factor_of
    return jnp.minimum(jnp.maximum(array, -bound), bound).astype(held_as)


def setup_inputs(seed: int = 0) -> dict:
    splits = jax.random.split(jax.random.key(seed), 10)
    tokens = draw_tokens(jax.random.fold_in(splits[9], 71), 0)
    doc_lengths = jax.vmap(lambda own: ragged_sizes(own, DOCS, TOK_DEV, DOC_MOST, 2))(jax.random.split(splits[1], SEQS)).reshape((SEQS, DOCS)).astype(jnp.int32)
    w_query = draw_w_query(jax.random.fold_in(splits[9], 71), 0)
    w_key = draw_w_key(jax.random.fold_in(splits[9], 71), 0)
    w_value = noise(splits[4], (D, KW), D ** -0.5, 0.0625, ((0, 8), (1, 4)))
    u_query = noise(splits[5], (QW,), 1.0, 6.0, ((0, 4),), jnp.float32)
    u_key = noise(splits[6], (KW,), 1.0, 6.0, ((0, 4),), jnp.float32)
    u_value = noise(splits[7], (KW,), 1.0, 6.0, ((0, 4),), jnp.float32)
    gammas = jnp.clip(jax.random.uniform(splits[8], (3,), jnp.float32, 0.5, 2.0), 0.5, 2.0)
    return dict(tokens=tokens, doc_lengths=doc_lengths, w_query=w_query, w_key=w_key, w_value=w_value, u_query=u_query, u_key=u_key, u_value=u_value, gammas=gammas)


EPSILON = 1e-12
HIGHEST = lax.Precision.HIGHEST
MASKED = -1e+30

def power_step(matrix, vector):
    widened = matrix.astype(jnp.float32)
    image = jnp.dot(widened, vector, precision=HIGHEST)
    unit = image * lax.rsqrt(jnp.sum(image * image) + EPSILON)
    backed = jnp.dot(unit, widened, precision=HIGHEST)
    sigma = jnp.sqrt(jnp.sum(backed * backed) + EPSILON)
    return (backed * (jnp.sqrt(jnp.float32(backed.shape[0])) / sigma), sigma)

def attention(queries, key_heads, value_heads, lengths):
    tok_rows = queries.shape[0]
    scores = jnp.einsum('tkgd,skd->kgts', queries.astype(jnp.float32), key_heads.astype(jnp.float32)) * HD ** (-0.5)
    doc_ends = jnp.cumsum(lengths)
    position = jnp.arange(tok_rows, dtype=jnp.int32)
    doc_ids = lax.optimization_barrier(jnp.sum((position[:, None] >= doc_ends[None, :]).astype(jnp.int32), axis=1))
    allowed = (doc_ids[:, None] == doc_ids[None, :]) & (position[None, :] <= position[:, None])
    scores = jnp.where(allowed, scores, MASKED)
    row_max = lax.optimization_barrier(jnp.max(scores, axis=-1, keepdims=True))
    exponent = jnp.exp(scores - row_max)
    attn_probs = (exponent / lax.optimization_barrier(jnp.sum(exponent, axis=-1, keepdims=True))).astype(jnp.bfloat16)
    mixed = jnp.einsum('kgts,skd->tkgd', attn_probs.astype(jnp.float32), value_heads.astype(jnp.float32))
    return mixed.astype(jnp.bfloat16).reshape(tok_rows, -1)

def reference(tokens, doc_lengths, w_query, w_key, w_value, u_query, u_key, u_value, gammas):
    query_pair = power_step(w_query, u_query)
    key_pair = power_step(w_key, u_key)
    value_pair = power_step(w_value, u_value)
    sigmas = jnp.stack([query_pair[1], key_pair[1], value_pair[1]])

    def projection(matrix, which):
        product = jnp.dot(tokens, matrix, preferred_element_type=jnp.float32)
        return (gammas[which] / sigmas[which] * product).astype(jnp.bfloat16)
    per_group = HEADS // KV_HEADS
    queries = projection(w_query, 0).reshape(SEQS, TOK_DEV, KV_HEADS, per_group, HD)
    key_heads = projection(w_key, 1).reshape(SEQS, TOK_DEV, KV_HEADS, HD)
    value_heads = projection(w_value, 2).reshape(SEQS, TOK_DEV, KV_HEADS, HD)
    context = lax.map(lambda operands: attention(*operands), (queries, key_heads, value_heads, doc_lengths))
    return (context.reshape(TOKENS, HEADS * HD), query_pair[0], key_pair[0], value_pair[0], sigmas)
```

```python
import functools

import jax
import jax.numpy as jnp
from jax import lax
from jax.experimental import pallas as pl
from jax.experimental.pallas import tpu as pltpu
from jax.sharding import PartitionSpec as P

HEADS = 32
KV_HEADS = 4
HD = 128
DOC_MOST = 192

EPSILON = 1e-12
HIGHEST = lax.Precision.HIGHEST
MASKED = -1e30
ROWS = ("rep", "fsdp")
F32 = jnp.float32
SMALL = pl.CostEstimate(flops=1, bytes_accessed=1, transcendentals=0)
BF16 = jnp.bfloat16
HALF = jnp.float16


def attention(queries, key_heads, value_heads, lengths):
    tok_rows = queries.shape[0]
    scores = jnp.einsum(
        "tkgd,skd->kgts", queries, key_heads, preferred_element_type=F32
    ) * queries.shape[-1] ** (-0.5)
    doc_ends = jnp.cumsum(lengths)
    position = jnp.arange(tok_rows, dtype=jnp.int32)
    doc_ids = jnp.sum((position[:, None] >= doc_ends[None, :]).astype(jnp.int32), axis=1)
    allowed = (doc_ids[:, None] == doc_ids[None, :]) & (position[None, :] <= position[:, None])
    scores = jnp.where(allowed, scores, MASKED)
    row_max = jnp.max(scores, axis=-1, keepdims=True)
    exponent = jnp.exp(scores - row_max)
    attn_probs = (exponent / jnp.sum(exponent, axis=-1, keepdims=True)).astype(BF16)
    mixed = jnp.einsum("kgts,skd->tkgd", attn_probs, value_heads, preferred_element_type=F32)
    return mixed.astype(BF16).reshape(tok_rows, -1)


def gather_body(tokens, doc_lengths, w_query, w_key, w_value, u_query, u_key, u_value, gammas):
    tok_rows = tokens.shape[0]
    widened = [w_query.astype(F32), w_key.astype(F32), w_value.astype(F32)]
    local_images = [
        jnp.dot(matrix, vector, precision=HIGHEST)
        for matrix, vector in zip(widened, (u_query, u_key, u_value))
    ]
    images = lax.psum((local_images[0], local_images[1], local_images[2]), "tp")
    squares = [jnp.sum(image * image) for image in images]
    norms = lax.psum((squares[0], squares[1], squares[2]), ROWS)
    partial_backs = [
        jnp.dot(image * lax.rsqrt(total_sq + EPSILON), matrix, precision=HIGHEST)
        for image, total_sq, matrix in zip(images, norms, widened)
    ]
    backs = lax.psum((partial_backs[0], partial_backs[1], partial_backs[2]), ROWS)
    back_sq = lax.psum(tuple(jnp.sum(back * back) for back in backs), "tp")
    sigma_list = [jnp.sqrt(total_sq + EPSILON) for total_sq in back_sq]
    tp_count = lax.axis_size("tp")
    new_states = [
        backed * (jnp.sqrt(F32(backed.shape[0] * tp_count)) / sigma)
        for backed, sigma in zip(backs, sigma_list)
    ]
    sigmas = jnp.stack(sigma_list)
    products = [
        jnp.dot(
            tokens, lax.all_gather(w, ROWS, axis=0, tiled=True), preferred_element_type=F32
        )
        for w in (w_query, w_key, w_value)
    ]
    scales = gammas / sigmas
    scaled = [(scales[which] * products[which]).astype(BF16) for which in range(3)]
    per_group = HEADS // KV_HEADS
    queries = scaled[0].reshape(tok_rows, -1, per_group, HD)
    key_heads = scaled[1].reshape(tok_rows, -1, HD)
    value_heads = scaled[2].reshape(tok_rows, -1, HD)
    context = attention(queries, key_heads, value_heads, doc_lengths[0])
    return (context, new_states[0], new_states[1], new_states[2], sigmas)


def stacked_terms(row):
    high = row.astype(BF16).astype(F32)
    rest = row - high
    middle = rest.astype(BF16).astype(F32)
    low = rest - middle
    which = lax.broadcasted_iota(jnp.int32, (8, row.shape[1]), 0)
    zero = jnp.zeros((8, row.shape[1]), F32)
    out = jnp.where(which == 0, high, jnp.where(which == 1, middle, jnp.where(which == 2, low, zero)))
    return out.astype(BF16)


def image_kernel(wq, wk, wv, uq, uk, uv, out):
    for i, (w, u) in enumerate(((wq, uq), (wk, uk), (wv, uv))):
        terms = lax.dot_general(
            stacked_terms(u[...]), w[...], (((1,), (1,)), ((), ())), preferred_element_type=F32
        )
        out[i : i + 1, :] = jnp.sum(terms, axis=0, keepdims=True)


def back_kernel(wq, wk, wv, image, out):
    lane = lax.broadcasted_iota(jnp.int32, (1, 128), 1)
    norms = jnp.zeros((1, 128), F32)
    at = 0
    for i, w in enumerate((wq, wk, wv)):
        row = image[i : i + 1, :]
        terms = jnp.dot(stacked_terms(row), w[...], preferred_element_type=F32)
        out[:, at : at + w.shape[1]] = jnp.sum(terms, axis=0, keepdims=True)
        at += w.shape[1]
        norms = jnp.where(lane == i, jnp.sum(row * row, axis=1, keepdims=True), norms)
    out[:, at : at + 128] = norms


def length_kernel(widths, summed, back, squares):
    lane = lax.broadcasted_iota(jnp.int32, (1, 128), 1)
    total = sum(widths)
    found = jnp.zeros((1, 128), F32)
    at = 0
    for i, width in enumerate(widths):
        norm = summed[:, total + i : total + i + 1]
        row = summed[:, at : at + width] * lax.rsqrt(norm + EPSILON)
        back[:, at : at + width] = row
        found = jnp.where(lane == i, jnp.sum(row * row, axis=1, keepdims=True), found)
        at += width
    squares[...] = found


def state_kernel(widths, tp_count, back, squares, new_q, new_k, new_v, sigmas):
    sigma = jnp.sqrt(squares[...] + EPSILON)
    sigmas[...] = sigma
    at = 0
    for i, (width, out) in enumerate(zip(widths, (new_q, new_k, new_v))):
        factor = jnp.sqrt(jnp.full((1, 1), width * tp_count, F32)) / sigma[:, i : i + 1]
        out[...] = back[:, at : at + width] * factor
        at += width


def whole(kernel, out_shape, *args):
    return pl.pallas_call(kernel, out_shape=out_shape, cost_estimate=SMALL)(*args)


def quarter_product(where, sources, w_own, w_other, index=None):
    deep, n = w_own.shape
    step = 512
    half = deep // step
    rows = sources[0].shape[0] if index is None else index[0]
    maps = [lambda k, where: (0, k)] * 4 if index is None else index[1](half)

    def kernel(where_ref, q0, q1, q2, q3, wa, wb, out):
        k = pl.program_id(0)
        x = jnp.concatenate([q[...] for q in (q0, q1, q2, q3)], axis=0)

        @pl.when(k == 0)
        def _():
            out[...] = jnp.dot(x, wa[...], preferred_element_type=F32)

        @pl.when((k > 0) & (k < half))
        def _():
            out[...] += jnp.dot(x, wa[...], preferred_element_type=F32)

        @pl.when(k >= half)
        def _():
            out[...] += jnp.dot(x, wb[...], preferred_element_type=F32)

    return pl.pallas_call(
        kernel,
        out_shape=jax.ShapeDtypeStruct((4 * rows, n), F32),
        grid_spec=pltpu.PrefetchScalarGridSpec(
            num_scalar_prefetch=1,
            grid=(2 * half,),
            in_specs=[pl.BlockSpec((rows, step), m) for m in maps]
            + [
                pl.BlockSpec((step, n), lambda k, where: (jnp.minimum(k, half - 1), 0)),
                pl.BlockSpec((step, n), lambda k, where: (jnp.maximum(k - half, 0), 0)),
            ],
            out_specs=pl.BlockSpec((4 * rows, n), lambda k, where: (0, 0)),
        ),
        cost_estimate=SMALL,
    )(where, *sources, w_own, w_other)


def context_kernel(first, heads, place, lengths, packed, *refs):
    if first:
        ctx, keys, values, scaled = refs
    else:
        keys, values, _, ctx, scaled = refs
    rows = packed.shape[0]
    block = rows // 4
    at = 2 * HD if first else 0
    for j in range(4):
        here = pl.ds(j * block, block)
        there = pl.ds(pl.multiple_of((place[0] ^ j) * block, block), block)
        if first:
            keys[there, :] = packed[here, :HD]
            values[there, :] = packed[here, HD:at]
        for h in range(heads):
            scaled[h, there, :] = packed[here, at + h * HD : at + (h + 1) * HD]
    for i in range(rows // block):
        low = max(0, (i * block - DOC_MOST + 1) // HD * HD)
        high = (i + 1) * block
        position = lax.broadcasted_iota(jnp.int32, (block, 1), 0) + i * block
        start = jnp.zeros((block, 1), jnp.int32)
        end = 0
        for k in range(lengths.shape[1]):
            end = end + lengths[0, k]
            start = jnp.where(position >= end, end, start)
        key_at = lax.broadcasted_iota(jnp.int32, (block, high - low), 1) + low
        allowed = ((key_at >= start) & (key_at <= position))[None]
        q = scaled[:, i * block : high, :].reshape(heads * block, HD)
        s = lax.dot_general(
            q, keys[low:high, :], (((1,), (1,)), ((), ())), preferred_element_type=F32
        ).reshape(heads, block, high - low)
        s = jnp.where(allowed, s * HD ** (-0.5), MASKED)
        e = jnp.exp(s - jnp.max(s, axis=2, keepdims=True))
        p = (e * (1.0 / jnp.sum(e, axis=2, keepdims=True))).astype(BF16)
        mixed = jnp.dot(
            p.reshape(heads * block, high - low), values[low:high, :], preferred_element_type=F32
        ).astype(BF16)
        for h in range(heads):
            ctx[i * block : high, h * HD : (h + 1) * HD] = mixed[h * block : (h + 1) * block, :]


def full(x):
    return pl.BlockSpec(x.shape, lambda i, place: (0,) * x.ndim)


def context_call(place, lengths, packed, width, kv=None, ctx=None):
    first = kv is None
    rows, n = packed.shape
    heads = (n - (2 * HD if first else 0)) // HD
    args = [lengths, packed]
    specs = [pl.BlockSpec(memory_space=pltpu.SMEM), full(packed)]
    half = jax.ShapeDtypeStruct((rows, HD), BF16)
    context = jax.ShapeDtypeStruct((rows, width), BF16)
    aliases = {}
    if first:
        out_shape = (context, half, half)
        out_specs = (
            pl.BlockSpec((rows, heads * HD), lambda i, place: (0, 0)),
            full(half),
            full(half),
        )
    else:
        args += [kv[0], kv[1], ctx]
        specs += [full(kv[0]), full(kv[1]), pl.BlockSpec(memory_space=pl.ANY)]
        out_shape = context
        out_specs = pl.BlockSpec((rows, heads * HD), lambda i, place: (0, 1))
        aliases = {len(args): 0}
    return pl.pallas_call(
        functools.partial(context_kernel, first, heads),
        out_shape=out_shape,
        grid_spec=pltpu.PrefetchScalarGridSpec(
            num_scalar_prefetch=1,
            grid=(1,),
            in_specs=specs,
            out_specs=out_specs,
            scratch_shapes=[pltpu.VMEM((heads, rows, HD), BF16)],
        ),
        input_output_aliases=aliases,
        cost_estimate=SMALL,
    )(place, *args)


class Order:
    def __init__(self):
        self.last = None

    def after(self, x):
        if self.last is None:
            return x
        x, self.last = lax.optimization_barrier((x, self.last))
        return x

    def note(self, x):
        self.last = x
        return x


def line_body(tokens, doc_lengths, w_query, w_key, w_value, u_query, u_key, u_value, gammas):
    tok_rows = tokens.shape[0]
    deep, q_width = w_query.shape
    kv_width = w_key.shape[1]
    widths = (q_width, kv_width, kv_width)
    reps, line, tp_count = lax.axis_size("rep"), lax.axis_size("fsdp"), lax.axis_size("tp")
    rep, slot, place = lax.axis_index("rep"), lax.axis_index("fsdp"), lax.axis_index("tp")
    quarter = tok_rows // tp_count
    send = lax.ppermute
    ends, mids, everyone = (0, line - 1), (1, line - 2), tuple(range(line))
    order = Order()
    after, note = order.after, order.note

    def swap(x, axis, mask, size):
        return send(x, axis, [(i, i ^ mask) for i in range(size)])

    def swap_tp(x, mask, who):
        pairs = [(s * tp_count + i, s * tp_count + (i ^ mask)) for s in who for i in range(tp_count)]
        return send(x, ("fsdp", "tp"), pairs)

    def cut(source, row, mask, rows):
        return jnp.concatenate(
            [
                lax.dynamic_slice(
                    source, (row, ((rep ^ r) * line + (slot ^ mask)) * deep), (rows, deep)
                )
                for r in range(reps)
            ],
            axis=1,
        )

    def product(parts, c):
        parts = after(tuple(parts))
        return note(quarter_product(where, parts, own_w[c], other_w[c]))

    def own_product(c):
        def maps(half):
            def one(j):
                def index(k, where):
                    column = ((where[1] ^ (k // half)) * line + where[2]) * half + k % half
                    return (where[0] ^ j, column)

                return index

            return [one(j) for j in range(tp_count)]

        source = after(tokens)
        return note(
            quarter_product(where, [source] * 4, own_w[c], other_w[c], (quarter, maps))
        )

    def arrived(x):
        return note(after(x))

    def joined(p, x):
        return note((p + after(x).astype(F32)).astype(HALF))

    def out(x):
        return send(x, "fsdp", [(0, 1), (3, 2)])

    def across(x):
        return send(x, "fsdp", [(1, 2), (2, 1)])

    where = jnp.stack([place, rep, slot]).astype(jnp.int32)
    split = q_width // 2
    total = sum(widths)
    row = jax.ShapeDtypeStruct((1, total), F32)
    lanes = jax.ShapeDtypeStruct((1, 128), F32)
    other_w = [None, None]

    mine = note(cut(tokens, place * quarter, 3, quarter))
    x3e = send(mine, "fsdp", [(0, 3), (3, 0)])
    own_w = [
        note(jnp.concatenate([after(w_key), w_value, w_query[:, :split]], axis=1)),
        w_query[:, split:],
    ]
    other_w[0] = swap(own_w[0], "rep", 1, reps)
    img = note(
        whole(
            image_kernel,
            jax.ShapeDtypeStruct((3, deep), F32),
            after(w_query),
            w_key,
            w_value,
            u_query[None],
            u_key[None],
            u_value[None],
        )
    )
    img_c = swap(img, "tp", 1, tp_count)
    x2 = note(cut(after(tokens), place * quarter, 2, quarter))
    img = note(img + after(img_c))
    img_y = swap(img, "tp", 2, tp_count)
    x2 = swap(after(x2), "fsdp", 2, line)
    x1 = note(cut(after(tokens), place * quarter, 1, quarter))
    img = note(img + after(img_y))
    back = note(
        whole(
            back_kernel,
            jax.ShapeDtypeStruct((1, total + 128), F32),
            w_query,
            w_key,
            w_value,
            after(img),
        )
    )
    x3e = arrived(x3e)
    x3e_far = swap_tp(x3e, 2, ends)
    x3e_near = swap_tp(x3e, 1, ends)
    x1 = swap(after(x1), "fsdp", 1, line)
    x3e_near = arrived(x3e_near)
    x3e_far = arrived(x3e_far)
    parts3e = (x3e, x3e_near, x3e_far, arrived(swap_tp(x3e_far, 1, ends)))
    other_w[0] = arrived(other_w[0])
    v = note(product(parts3e, 0).astype(HALF))
    a3 = out(v)
    back_x = swap(after(back), "rep", 1, reps)
    x2 = arrived(x2)
    x2_far = swap_tp(x2, 2, everyone)
    x2_near = arrived(swap_tp(x2, 1, everyone))
    back = note(back + after(back_x))
    back_z = swap(back, "fsdp", 1, line)
    other_w[1] = swap(after(own_w[1]), "rep", 1, reps)
    x1 = arrived(x1)
    x3m = across(after(mine))
    p0 = [own_product(0), None]
    x2_far = arrived(x2_far)
    x1_far = swap_tp(after(x1), 2, everyone)
    parts2 = (x2, x2_near, x2_far, arrived(swap_tp(x2_far, 1, everyone)))
    p2 = product(parts2, 0)
    x3m = arrived(x3m)
    x1_near = arrived(swap_tp(after(x1), 1, everyone))
    v = joined(p2, a3)
    a2e, a2m = out(v), across(v)
    back = note(back + after(back_z))
    back_z = swap(back, "fsdp", 2, line)
    x1_far = arrived(x1_far)
    parts1 = (x1, x1_near, x1_far, arrived(swap_tp(x1_far, 1, everyone)))
    p1 = product(parts1, 0)
    other_w[1] = arrived(other_w[1])
    v = note(product(parts3e, 1).astype(HALF))
    a3 = out(v)
    x3m_far = swap_tp(after(x3m), 2, mids)
    p2 = product(parts2, 1)
    x3m_far = arrived(x3m_far)
    x3m_near = swap_tp(after(x3m), 1, mids)
    x3m_last = swap_tp(x3m_far, 1, mids)
    parts3 = (x3m, arrived(x3m_near), x3m_far, arrived(x3m_last))
    p3 = product(parts3, 0)
    v = joined(p3, a2e)
    a1m = [across(v), None]
    v = joined(p1, a2m)
    a1p = [swap(v, "fsdp", 1, line), None]
    p1 = product(parts1, 1)
    back = note(back + after(back_z))
    back, squares = note(whole(functools.partial(length_kernel, widths), (row, lanes), back))
    squares_c = swap(squares, "tp", 1, tp_count)
    p3 = product(parts3, 1)
    squares = note(squares + after(squares_c))
    v = joined(p2, a3)
    a2e, a2m = out(v), across(v)
    squares_y = swap(after(squares), "tp", 2, tp_count)
    p0[1] = own_product(1)
    squares = note(squares + after(squares_y))
    states = note(
        whole(
            functools.partial(state_kernel, widths, tp_count),
            tuple(jax.ShapeDtypeStruct((1, n), F32) for n in widths) + (lanes,),
            back,
            squares,
        )
    )
    scales = gammas / states[3][0, :3]
    q_row = jnp.full((1, split), 1.0, F32) * scales[0]
    kv_row = [jnp.full((1, kv_width), 1.0, F32) * scales[i] for i in (1, 2)]
    factor = [jnp.concatenate(kv_row + [q_row], axis=1), q_row]
    factor = note(after(tuple(factor)))
    v = joined(p3, a2e)
    a1m[1] = across(v)
    v = joined(p1, a2m)
    a1p[1] = swap(v, "fsdp", 1, line)

    def packed(c):
        near, far = after((a1p[c], a1m[c]))
        return note((factor[c] * (p0[c] + near.astype(F32) + far.astype(F32))).astype(BF16))

    ctx, keys, values = note(context_call(where, doc_lengths, packed(0), q_width))
    context = context_call(where, doc_lengths, packed(1), q_width, (keys, values), ctx)
    return (context, states[0][0], states[1][0], states[2][0], states[3][0, :3])


def solution(mesh):
    in_specs = (
        P(("rep", "fsdp"), None),
        P(("rep", "fsdp"), None),
        P(("rep", "fsdp"), "tp"),
        P(("rep", "fsdp"), "tp"),
        P(("rep", "fsdp"), "tp"),
        P("tp"),
        P("tp"),
        P("tp"),
        P(),
    )
    out_specs = (P(("rep", "fsdp"), "tp"), P("tp"), P("tp"), P("tp"), P())
    sizes = tuple(mesh.shape[name] for name in ("rep", "fsdp", "tp"))
    body = line_body if sizes == (2, 4, 4) else gather_body
    return jax.shard_map(body, mesh=mesh, in_specs=in_specs, out_specs=out_specs, check_vma=False)
```

```python
import functools

import jax
import jax.numpy as jnp
from jax import lax
from jax.experimental import pallas as pl
from jax.experimental.pallas import tpu as pltpu
from jax.sharding import PartitionSpec as P

HEADS = 32
KV_HEADS = 4
HD = 128
DOC_MOST = 192

EPSILON = 1e-12
HIGHEST = lax.Precision.HIGHEST
MASKED = -1e30
ROWS = ("rep", "fsdp")
F32 = jnp.float32
SMALL = pl.CostEstimate(flops=1, bytes_accessed=1, transcendentals=0)
BF16 = jnp.bfloat16
HALF = jnp.float16


def attention(queries, key_heads, value_heads, lengths):
    tok_rows = queries.shape[0]
    scores = jnp.einsum(
        "tkgd,skd->kgts", queries, key_heads, preferred_element_type=F32
    ) * queries.shape[-1] ** (-0.5)
    doc_ends = jnp.cumsum(lengths)
    position = jnp.arange(tok_rows, dtype=jnp.int32)
    doc_ids = jnp.sum((position[:, None] >= doc_ends[None, :]).astype(jnp.int32), axis=1)
    allowed = (doc_ids[:, None] == doc_ids[None, :]) & (position[None, :] <= position[:, None])
    scores = jnp.where(allowed, scores, MASKED)
    row_max = jnp.max(scores, axis=-1, keepdims=True)
    exponent = jnp.exp(scores - row_max)
    attn_probs = (exponent / jnp.sum(exponent, axis=-1, keepdims=True)).astype(BF16)
    mixed = jnp.einsum("kgts,skd->tkgd", attn_probs, value_heads, preferred_element_type=F32)
    return mixed.astype(BF16).reshape(tok_rows, -1)


def gather_body(tokens, doc_lengths, w_query, w_key, w_value, u_query, u_key, u_value, gammas):
    tok_rows = tokens.shape[0]
    widened = [w_query.astype(F32), w_key.astype(F32), w_value.astype(F32)]
    local_images = [
        jnp.dot(matrix, vector, precision=HIGHEST)
        for matrix, vector in zip(widened, (u_query, u_key, u_value))
    ]
    images = lax.psum((local_images[0], local_images[1], local_images[2]), "tp")
    squares = [jnp.sum(image * image) for image in images]
    norms = lax.psum((squares[0], squares[1], squares[2]), ROWS)
    partial_backs = [
        jnp.dot(image * lax.rsqrt(total_sq + EPSILON), matrix, precision=HIGHEST)
        for image, total_sq, matrix in zip(images, norms, widened)
    ]
    backs = lax.psum((partial_backs[0], partial_backs[1], partial_backs[2]), ROWS)
    back_sq = lax.psum(tuple(jnp.sum(back * back) for back in backs), "tp")
    sigma_list = [jnp.sqrt(total_sq + EPSILON) for total_sq in back_sq]
    tp_count = lax.axis_size("tp")
    new_states = [
        backed * (jnp.sqrt(F32(backed.shape[0] * tp_count)) / sigma)
        for backed, sigma in zip(backs, sigma_list)
    ]
    sigmas = jnp.stack(sigma_list)
    products = [
        jnp.dot(
            tokens, lax.all_gather(w, ROWS, axis=0, tiled=True), preferred_element_type=F32
        )
        for w in (w_query, w_key, w_value)
    ]
    scales = gammas / sigmas
    scaled = [(scales[which] * products[which]).astype(BF16) for which in range(3)]
    per_group = HEADS // KV_HEADS
    queries = scaled[0].reshape(tok_rows, -1, per_group, HD)
    key_heads = scaled[1].reshape(tok_rows, -1, HD)
    value_heads = scaled[2].reshape(tok_rows, -1, HD)
    context = attention(queries, key_heads, value_heads, doc_lengths[0])
    return (context, new_states[0], new_states[1], new_states[2], sigmas)


def stacked_terms(row):
    high = row.astype(BF16).astype(F32)
    rest = row - high
    middle = rest.astype(BF16).astype(F32)
    low = rest - middle
    which = lax.broadcasted_iota(jnp.int32, (8, row.shape[1]), 0)
    zero = jnp.zeros((8, row.shape[1]), F32)
    out = jnp.where(which == 0, high, jnp.where(which == 1, middle, jnp.where(which == 2, low, zero)))
    return out.astype(BF16)


def image_kernel(wq, wk, wv, uq, uk, uv, out):
    for i, (w, u) in enumerate(((wq, uq), (wk, uk), (wv, uv))):
        terms = lax.dot_general(
            stacked_terms(u[...]), w[...], (((1,), (1,)), ((), ())), preferred_element_type=F32
        )
        out[i : i + 1, :] = jnp.sum(terms, axis=0, keepdims=True)


def back_kernel(wq, wk, wv, image, out):
    lane = lax.broadcasted_iota(jnp.int32, (1, 128), 1)
    norms = jnp.zeros((1, 128), F32)
    at = 0
    for i, w in enumerate((wq, wk, wv)):
        row = image[i : i + 1, :]
        terms = jnp.dot(stacked_terms(row), w[...], preferred_element_type=F32)
        out[:, at : at + w.shape[1]] = jnp.sum(terms, axis=0, keepdims=True)
        at += w.shape[1]
        norms = jnp.where(lane == i, jnp.sum(row * row, axis=1, keepdims=True), norms)
    out[:, at : at + 128] = norms


def length_kernel(widths, summed, back, squares):
    lane = lax.broadcasted_iota(jnp.int32, (1, 128), 1)
    total = sum(widths)
    found = jnp.zeros((1, 128), F32)
    at = 0
    for i, width in enumerate(widths):
        norm = summed[:, total + i : total + i + 1]
        row = summed[:, at : at + width] * lax.rsqrt(norm + EPSILON)
        back[:, at : at + width] = row
        found = jnp.where(lane == i, jnp.sum(row * row, axis=1, keepdims=True), found)
        at += width
    squares[...] = found


def state_kernel(widths, tp_count, back, squares, gammas, new_q, new_k, new_v, sigmas, factors):
    sigma = jnp.sqrt(squares[...] + EPSILON)
    sigmas[...] = sigma
    for i, (start, width) in enumerate(
        ((2 * widths[1], widths[0]), (0, widths[1]), (widths[1], widths[2]))
    ):
        factors[:, start : start + width] = jnp.broadcast_to(
            gammas[i] / sigma[:, i : i + 1], (1, width)
        )
    at = 0
    for i, (width, out) in enumerate(zip(widths, (new_q, new_k, new_v))):
        factor = jnp.sqrt(jnp.full((1, 1), width * tp_count, F32)) / sigma[:, i : i + 1]
        out[...] = back[:, at : at + width] * factor
        at += width


def whole(kernel, out_shape, *args):
    specs = [
        pl.BlockSpec(memory_space=pltpu.SMEM if a.ndim == 1 else pltpu.VMEM) for a in args
    ]
    return pl.pallas_call(kernel, out_shape=out_shape, in_specs=specs, cost_estimate=SMALL)(*args)


def gather_blocks(where, sources, outs, plan):
    count = len(plan([0, 0, 0]))
    n = len(sources)

    def kernel(where_ref, *refs):
        sems = refs[-1]
        place = [where_ref[i] for i in range(3)]
        copies = [
            pltpu.make_async_copy(refs[s].at[at], refs[n + o].at[to], sems.at[i])
            for i, (s, at, o, to) in enumerate(plan(place))
        ]
        for copy in copies:
            copy.start()
        for copy in copies:
            copy.wait()

    anywhere = pl.BlockSpec(memory_space=pl.ANY)
    return pl.pallas_call(
        kernel,
        out_shape=outs,
        grid_spec=pltpu.PrefetchScalarGridSpec(
            num_scalar_prefetch=1,
            grid=(1,),
            in_specs=[anywhere] * n,
            out_specs=tuple(pl.BlockSpec(o.shape, lambda i, where: (0, 0)) for o in outs),
            scratch_shapes=[pltpu.SemaphoreType.DMA((count,))],
        ),
        cost_estimate=SMALL,
    )(where, *sources)


def context_kernel(first, heads, place, lengths, packed, *refs):
    if first:
        ctx, keys, values, scaled = refs
    else:
        keys, values, _, ctx, scaled = refs
    rows = packed.shape[0]
    block = rows // 4
    at = 2 * HD if first else 0
    for i, j in enumerate((0, 2, 1, 3)):
        here = pl.ds(i * block, block)
        there = pl.ds(pl.multiple_of((place[0] ^ j) * block, block), block)
        if first:
            keys[there, :] = packed[here, :HD]
            values[there, :] = packed[here, HD:at]
        for h in range(heads):
            scaled[h, there, :] = packed[here, at + h * HD : at + (h + 1) * HD]
    for i in range(rows // block):
        low = max(0, (i * block - DOC_MOST + 1) // HD * HD)
        high = (i + 1) * block
        position = lax.broadcasted_iota(jnp.int32, (block, 1), 0) + i * block
        start = jnp.zeros((block, 1), jnp.int32)
        end = 0
        for k in range(lengths.shape[1]):
            end = end + lengths[0, k]
            start = jnp.where(position >= end, end, start)
        key_at = lax.broadcasted_iota(jnp.int32, (block, high - low), 1) + low
        allowed = ((key_at >= start) & (key_at <= position))[None]
        q = scaled[:, i * block : high, :].reshape(heads * block, HD)
        s = lax.dot_general(
            q, keys[low:high, :], (((1,), (1,)), ((), ())), preferred_element_type=F32
        ).reshape(heads, block, high - low)
        s = jnp.where(allowed, s * HD ** (-0.5), MASKED)
        e = jnp.exp(s - jnp.max(s, axis=2, keepdims=True))
        p = (e * (1.0 / jnp.sum(e, axis=2, keepdims=True))).astype(BF16)
        mixed = jnp.dot(
            p.reshape(heads * block, high - low), values[low:high, :], preferred_element_type=F32
        ).astype(BF16)
        for h in range(heads):
            ctx[i * block : high, h * HD : (h + 1) * HD] = mixed[h * block : (h + 1) * block, :]


def full(x):
    return pl.BlockSpec(x.shape, lambda i, place: (0,) * x.ndim)


def context_call(place, lengths, packed, width, kv=None, ctx=None):
    first = kv is None
    rows, n = packed.shape
    heads = (n - (2 * HD if first else 0)) // HD
    args = [lengths, packed]
    specs = [pl.BlockSpec(memory_space=pltpu.SMEM), full(packed)]
    half = jax.ShapeDtypeStruct((rows, HD), BF16)
    context = jax.ShapeDtypeStruct((rows, width), BF16)
    aliases = {}
    if first:
        out_shape = (context, half, half)
        out_specs = (
            pl.BlockSpec((rows, heads * HD), lambda i, place: (0, 0)),
            full(half),
            full(half),
        )
    else:
        args += [kv[0], kv[1], ctx]
        specs += [full(kv[0]), full(kv[1]), pl.BlockSpec(memory_space=pl.ANY)]
        out_shape = context
        out_specs = pl.BlockSpec((rows, heads * HD), lambda i, place: (0, 1))
        aliases = {len(args): 0}
    return pl.pallas_call(
        functools.partial(context_kernel, first, heads),
        out_shape=out_shape,
        grid_spec=pltpu.PrefetchScalarGridSpec(
            num_scalar_prefetch=1,
            grid=(1,),
            in_specs=specs,
            out_specs=out_specs,
            scratch_shapes=[pltpu.VMEM((heads, rows, HD), BF16)],
        ),
        input_output_aliases=aliases,
        cost_estimate=SMALL,
    )(place, *args)


class Order:
    def __init__(self, token):
        self.token = token

    def after(self, x):
        x, self.token = lax.optimization_barrier((x, self.token))
        return x

    note = after


def line_body(tokens, doc_lengths, w_query, w_key, w_value, u_query, u_key, u_value, gammas):
    deep, q_width = w_query.shape
    kv_width = w_key.shape[1]
    widths = (q_width, kv_width, kv_width)
    reps, line, tp_count = lax.axis_size("rep"), lax.axis_size("fsdp"), lax.axis_size("tp")
    rep, slot, place = lax.axis_index("rep"), lax.axis_index("fsdp"), lax.axis_index("tp")
    send = lax.ppermute
    where = jnp.stack([place, rep, slot]).astype(jnp.int32)
    ends, mids, everyone = (0, line - 1), (1, line - 2), tuple(range(line))
    order = Order(doc_lengths)
    after, note = order.after, order.note

    def swap(x, axis, mask, size):
        return send(x, axis, [(i, i ^ mask) for i in range(size)])

    def swap_tp(x, mask, who):
        pairs = [(s * tp_count + i, s * tp_count + (i ^ mask)) for s in who for i in range(tp_count)]
        return send(x, ("fsdp", "tp"), pairs)

    quarter = tokens.shape[0] // tp_count

    def slab(source, mask, out, flips):
        def plan(at):
            return [
                (
                    source,
                    (
                        pl.ds(pl.multiple_of((at[0] ^ flip) * quarter, quarter), quarter),
                        pl.ds(
                            pl.multiple_of(((at[1] ^ r) * line + (at[2] ^ mask)) * deep, deep), deep
                        ),
                    ),
                    out,
                    (pl.ds(j * quarter, quarter), pl.ds(r * deep, deep)),
                )
                for j, flip in enumerate(flips)
                for r in range(reps)
            ]

        return plan

    def piece(rows, columns):
        return jax.ShapeDtypeStruct((rows, columns), BF16)

    def product(x, w):
        return jnp.dot(x[:, :deep], w[0], preferred_element_type=F32) + jnp.dot(
            x[:, deep:], w[1], preferred_element_type=F32
        )

    def arrived(x):
        return note(x)

    def out(x):
        return send(x, "fsdp", [(0, 1), (3, 2)])

    def across(x):
        return send(x, "fsdp", [(1, 2), (2, 1)])

    split = q_width // 2
    wide = 2 * kv_width + split
    total = sum(widths)
    row = jax.ShapeDtypeStruct((1, total), F32)
    lanes = jax.ShapeDtypeStruct((1, 128), F32)

    every = pl.ds(0, deep)
    own_w = [None, None]
    mine, own_w[0] = note(
        gather_blocks(
            where,
            (tokens, w_key, w_value, w_query),
            (piece(quarter, reps * deep), piece(deep, wide)),
            lambda at: slab(0, 3, 0, (0,))(at)
            + [
                (1, (every, pl.ds(0, kv_width)), 1, (every, pl.ds(0, kv_width))),
                (2, (every, pl.ds(0, kv_width)), 1, (every, pl.ds(kv_width, kv_width))),
                (3, (every, pl.ds(0, split)), 1, (every, pl.ds(2 * kv_width, split))),
            ],
        )
    )
    x3e = send(mine, "fsdp", [(0, 3), (3, 0)])
    other_w = [swap(own_w[0], "rep", 1, reps), None]
    x2, x1, own_w[1] = note(
        gather_blocks(
            after(where),
            (tokens, w_query),
            (piece(quarter, reps * deep), piece(quarter, reps * deep), piece(deep, split)),
            lambda at: slab(0, 2, 0, (0,))(at)
            + slab(0, 1, 1, (0,))(at)
            + [(1, (every, pl.ds(split, split)), 2, (every, pl.ds(0, split)))],
        )
    )
    x2 = swap(x2, "fsdp", 2, line)
    img = note(
        whole(
            image_kernel,
            jax.ShapeDtypeStruct((3, deep), F32),
            w_query,
            w_key,
            w_value,
            after(u_query[None] + 0.0),
            u_key[None],
            u_value[None],
        )
    )
    img = note(img + swap(img, "tp", 1, tp_count))
    img = note(img + swap(img, "tp", 2, tp_count))
    back = note(
        whole(
            back_kernel,
            jax.ShapeDtypeStruct((1, total + 128), F32),
            w_query,
            w_key,
            w_value,
            img,
        )
    )
    back_x = swap(back, "rep", 1, reps)

    def joint(a, b):
        return note(jnp.concatenate([a, after(b)], axis=0))

    def joined(p, x):
        return note((p + after(x).astype(F32)).astype(HALF))

    def summed(x, axis, size):
        parts = [swap(x, axis, mask, size) for mask in (1, 2, 3)]
        return lambda: note((x + after(parts[0])) + (parts[1] + parts[2]))

    x3e = arrived(x3e)
    y3e = swap_tp(x3e, 2, ends)
    x2 = arrived(x2)
    y2 = swap_tp(x2, 2, everyone)
    x1 = swap(after(x1), "fsdp", 1, line)
    x3m = across(after(mine))
    rows0 = note(
        gather_blocks(
            after(where),
            (tokens,),
            (piece(tp_count * quarter, reps * deep),),
            slab(0, 0, 0, (0, 2, 1, 3)),
        )[0]
    )
    pair = joint(x3e, y3e)
    c3e = swap_tp(pair, 1, ends)
    pair2 = joint(x2, y2)
    c2 = swap_tp(pair2, 1, everyone)
    w = [(own_w[0], arrived(other_w[0])), None]
    back = note(back + after(back_x))
    back_z = summed(back, "fsdp", line)
    rows3e = joint(pair, c3e)
    v = note(product(after(rows3e), w[0]).astype(HALF))
    back, squares = note(
        whole(functools.partial(length_kernel, widths), (row, lanes), back_z())
    )
    a3 = [out(after(v)), None]
    squares = summed(after(squares), "tp", tp_count)()
    states = note(
        whole(
            functools.partial(state_kernel, widths, tp_count),
            tuple(jax.ShapeDtypeStruct((1, n), F32) for n in widths) + (lanes, row),
            back,
            squares,
            gammas,
        )
    )
    factors = states[4]
    factor = [factors[:, :wide], factors[:, wide:]]
    x1 = arrived(x1)
    y1 = swap_tp(x1, 2, everyone)
    x3m = arrived(x3m)
    y3m = swap_tp(x3m, 2, mids)
    other_w[1] = swap(after(own_w[1]), "rep", 1, reps)
    rows2 = joint(pair2, c2)
    p2 = [note(product(after(rows2), w[0])), None]
    p0 = [note(product(after(rows0), w[0])), None]
    v = joined(p2[0], a3[0])
    a2e, a2m = [out(v), None], [across(v), None]
    pair1 = joint(x1, y1)
    c1 = swap_tp(pair1, 1, everyone)
    pair3 = joint(x3m, y3m)
    c3m = swap_tp(pair3, 1, mids)
    w[1] = (own_w[1], arrived(other_w[1]))
    a3[1] = out(note(product(after(rows3e), w[1]).astype(HALF)))
    p0[1] = note(product(after(rows0), w[1]))
    p2[1] = note(product(after(rows2), w[1]))
    rows1 = joint(pair1, c1)
    p1 = [note(product(after(rows1), w[c])) for c in range(2)]
    rows3m = joint(pair3, c3m)
    p3m = [note(product(after(rows3m), w[c])) for c in range(2)]
    a1p = [swap(joined(p1[0], a2m[0]), "fsdp", 1, line), None]
    a1m = [across(joined(p3m[0], a2e[0])), None]
    v = joined(p2[1], a3[1])
    a2e[1], a2m[1] = out(v), across(v)
    a1p[1] = swap(joined(p1[1], a2m[1]), "fsdp", 1, line)
    a1m[1] = across(joined(p3m[1], a2e[1]))

    def packed(c):
        near, far = after((a1p[c], a1m[c]))
        return note((factor[c] * (p0[c] + near.astype(F32) + far.astype(F32))).astype(BF16))

    first = packed(0)
    ctx, keys, values = note(context_call(where, order.token, first, q_width))
    second = packed(1)
    context = context_call(where, order.token, second, q_width, (keys, values), ctx)
    return (context, states[0][0], states[1][0], states[2][0], states[3][0, :3])


def solution(mesh):
    in_specs = (
        P(("rep", "fsdp"), None),
        P(("rep", "fsdp"), None),
        P(("rep", "fsdp"), "tp"),
        P(("rep", "fsdp"), "tp"),
        P(("rep", "fsdp"), "tp"),
        P("tp"),
        P("tp"),
        P("tp"),
        P(),
    )
    out_specs = (P(("rep", "fsdp"), "tp"), P("tp"), P("tp"), P("tp"), P())
    sizes = tuple(mesh.shape[name] for name in ("rep", "fsdp", "tp"))
    body = line_body if sizes == (2, 4, 4) else gather_body
    return jax.shard_map(body, mesh=mesh, in_specs=in_specs, out_specs=out_specs, check_vma=False)
```

```python
import functools

import jax
import jax.numpy as jnp
from jax import lax
from jax.experimental import pallas as pl
from jax.experimental.pallas import tpu as pltpu
from jax.sharding import PartitionSpec as P

HEADS = 32
KV_HEADS = 4
HD = 128
DOC_MOST = 192

EPSILON = 1e-12
HIGHEST = lax.Precision.HIGHEST
MASKED = -1e30
ROWS = ("rep", "fsdp")
F32 = jnp.float32
SMALL = pl.CostEstimate(flops=1, bytes_accessed=1, transcendentals=0)
BF16 = jnp.bfloat16
HALF = jnp.float16


def attention(queries, key_heads, value_heads, lengths):
    tok_rows = queries.shape[0]
    scores = jnp.einsum(
        "tkgd,skd->kgts", queries, key_heads, preferred_element_type=F32
    ) * queries.shape[-1] ** (-0.5)
    doc_ends = jnp.cumsum(lengths)
    position = jnp.arange(tok_rows, dtype=jnp.int32)
    doc_ids = jnp.sum((position[:, None] >= doc_ends[None, :]).astype(jnp.int32), axis=1)
    allowed = (doc_ids[:, None] == doc_ids[None, :]) & (position[None, :] <= position[:, None])
    scores = jnp.where(allowed, scores, MASKED)
    row_max = jnp.max(scores, axis=-1, keepdims=True)
    exponent = jnp.exp(scores - row_max)
    attn_probs = (exponent / jnp.sum(exponent, axis=-1, keepdims=True)).astype(BF16)
    mixed = jnp.einsum("kgts,skd->tkgd", attn_probs, value_heads, preferred_element_type=F32)
    return mixed.astype(BF16).reshape(tok_rows, -1)


def gather_body(tokens, doc_lengths, w_query, w_key, w_value, u_query, u_key, u_value, gammas):
    tok_rows = tokens.shape[0]
    widened = [w_query.astype(F32), w_key.astype(F32), w_value.astype(F32)]
    local_images = [
        jnp.dot(matrix, vector, precision=HIGHEST)
        for matrix, vector in zip(widened, (u_query, u_key, u_value))
    ]
    images = lax.psum((local_images[0], local_images[1], local_images[2]), "tp")
    squares = [jnp.sum(image * image) for image in images]
    norms = lax.psum((squares[0], squares[1], squares[2]), ROWS)
    partial_backs = [
        jnp.dot(image * lax.rsqrt(total_sq + EPSILON), matrix, precision=HIGHEST)
        for image, total_sq, matrix in zip(images, norms, widened)
    ]
    backs = lax.psum((partial_backs[0], partial_backs[1], partial_backs[2]), ROWS)
    back_sq = lax.psum(tuple(jnp.sum(back * back) for back in backs), "tp")
    sigma_list = [jnp.sqrt(total_sq + EPSILON) for total_sq in back_sq]
    tp_count = lax.axis_size("tp")
    new_states = [
        backed * (jnp.sqrt(F32(backed.shape[0] * tp_count)) / sigma)
        for backed, sigma in zip(backs, sigma_list)
    ]
    sigmas = jnp.stack(sigma_list)
    products = [
        jnp.dot(
            tokens, lax.all_gather(w, ROWS, axis=0, tiled=True), preferred_element_type=F32
        )
        for w in (w_query, w_key, w_value)
    ]
    scales = gammas / sigmas
    scaled = [(scales[which] * products[which]).astype(BF16) for which in range(3)]
    per_group = HEADS // KV_HEADS
    queries = scaled[0].reshape(tok_rows, -1, per_group, HD)
    key_heads = scaled[1].reshape(tok_rows, -1, HD)
    value_heads = scaled[2].reshape(tok_rows, -1, HD)
    context = attention(queries, key_heads, value_heads, doc_lengths[0])
    return (context, new_states[0], new_states[1], new_states[2], sigmas)


def stacked_terms(row):
    high = row.astype(BF16).astype(F32)
    rest = row - high
    middle = rest.astype(BF16).astype(F32)
    low = rest - middle
    which = lax.broadcasted_iota(jnp.int32, (8, row.shape[1]), 0)
    zero = jnp.zeros((8, row.shape[1]), F32)
    out = jnp.where(which == 0, high, jnp.where(which == 1, middle, jnp.where(which == 2, low, zero)))
    return out.astype(BF16)


def image_kernel(wq, wk, wv, uq, uk, uv, out):
    for i, (w, u) in enumerate(((wq, uq), (wk, uk), (wv, uv))):
        terms = lax.dot_general(
            stacked_terms(u[...]), w[...], (((1,), (1,)), ((), ())), preferred_element_type=F32
        )
        out[i : i + 1, :] = jnp.sum(terms, axis=0, keepdims=True)


def back_kernel(wq, wk, wv, image, out):
    lane = lax.broadcasted_iota(jnp.int32, (1, 128), 1)
    norms = jnp.zeros((1, 128), F32)
    at = 0
    for i, w in enumerate((wq, wk, wv)):
        row = image[i : i + 1, :]
        terms = jnp.dot(stacked_terms(row), w[...], preferred_element_type=F32)
        out[:, at : at + w.shape[1]] = jnp.sum(terms, axis=0, keepdims=True)
        at += w.shape[1]
        norms = jnp.where(lane == i, jnp.sum(row * row, axis=1, keepdims=True), norms)
    out[:, at : at + 128] = norms


def length_kernel(widths, summed, back, squares):
    lane = lax.broadcasted_iota(jnp.int32, (1, 128), 1)
    total = sum(widths)
    found = jnp.zeros((1, 128), F32)
    at = 0
    for i, width in enumerate(widths):
        norm = summed[:, total + i : total + i + 1]
        row = summed[:, at : at + width] * lax.rsqrt(norm + EPSILON)
        back[:, at : at + width] = row
        found = jnp.where(lane == i, jnp.sum(row * row, axis=1, keepdims=True), found)
        at += width
    squares[...] = found


def state_kernel(widths, tp_count, back, squares, gammas, new_q, new_k, new_v, sigmas, factors):
    sigma = jnp.sqrt(squares[...] + EPSILON)
    sigmas[...] = sigma
    for i, (start, width) in enumerate(
        ((2 * widths[1], widths[0]), (0, widths[1]), (widths[1], widths[2]))
    ):
        factors[:, start : start + width] = jnp.broadcast_to(
            gammas[i] / sigma[:, i : i + 1], (1, width)
        )
    at = 0
    for i, (width, out) in enumerate(zip(widths, (new_q, new_k, new_v))):
        factor = jnp.sqrt(jnp.full((1, 1), width * tp_count, F32)) / sigma[:, i : i + 1]
        out[...] = back[:, at : at + width] * factor
        at += width


def whole(kernel, out_shape, *args):
    specs = [
        pl.BlockSpec(memory_space=pltpu.SMEM if a.ndim == 1 else pltpu.VMEM) for a in args
    ]
    return pl.pallas_call(kernel, out_shape=out_shape, in_specs=specs, cost_estimate=SMALL)(*args)


def gather_blocks(where, sources, outs, plan):
    count = len(plan([0, 0, 0]))
    n = len(sources)

    def kernel(where_ref, *refs):
        sems = refs[-1]
        place = [where_ref[i] for i in range(3)]
        copies = [
            pltpu.make_async_copy(refs[s].at[at], refs[n + o].at[to], sems.at[i])
            for i, (s, at, o, to) in enumerate(plan(place))
        ]
        for copy in copies:
            copy.start()
        for copy in copies:
            copy.wait()

    anywhere = pl.BlockSpec(memory_space=pl.ANY)
    return pl.pallas_call(
        kernel,
        out_shape=outs,
        grid_spec=pltpu.PrefetchScalarGridSpec(
            num_scalar_prefetch=1,
            grid=(1,),
            in_specs=[anywhere] * n,
            out_specs=tuple(pl.BlockSpec(o.shape, lambda i, where: (0, 0)) for o in outs),
            scratch_shapes=[pltpu.SemaphoreType.DMA((count,))],
        ),
        cost_estimate=SMALL,
    )(where, *sources)


def context_kernel(first, heads, place, lengths, packed, *refs):
    if first:
        ctx, keys, values, scaled = refs
    else:
        keys, values, _, ctx, scaled = refs
    rows = packed.shape[0]
    block = rows // 4
    at = 2 * HD if first else 0
    for i, j in enumerate((0, 2, 1, 3)):
        here = pl.ds(i * block, block)
        there = pl.ds(pl.multiple_of((place[0] ^ j) * block, block), block)
        if first:
            keys[there, :] = packed[here, :HD]
            values[there, :] = packed[here, HD:at]
        for h in range(heads):
            scaled[h, there, :] = packed[here, at + h * HD : at + (h + 1) * HD]
    for i in range(rows // block):
        low = max(0, (i * block - DOC_MOST + 1) // HD * HD)
        high = (i + 1) * block
        position = lax.broadcasted_iota(jnp.int32, (block, 1), 0) + i * block
        start = jnp.zeros((block, 1), jnp.int32)
        end = 0
        for k in range(lengths.shape[1]):
            end = end + lengths[0, k]
            start = jnp.where(position >= end, end, start)
        key_at = lax.broadcasted_iota(jnp.int32, (block, high - low), 1) + low
        allowed = ((key_at >= start) & (key_at <= position))[None]
        q = scaled[:, i * block : high, :].reshape(heads * block, HD)
        s = lax.dot_general(
            q, keys[low:high, :], (((1,), (1,)), ((), ())), preferred_element_type=F32
        ).reshape(heads, block, high - low)
        s = jnp.where(allowed, s * HD ** (-0.5), MASKED)
        e = jnp.exp(s - jnp.max(s, axis=2, keepdims=True))
        p = (e * (1.0 / jnp.sum(e, axis=2, keepdims=True))).astype(BF16)
        mixed = jnp.dot(
            p.reshape(heads * block, high - low), values[low:high, :], preferred_element_type=F32
        ).astype(BF16)
        for h in range(heads):
            ctx[i * block : high, h * HD : (h + 1) * HD] = mixed[h * block : (h + 1) * block, :]


def full(x):
    return pl.BlockSpec(x.shape, lambda i, place: (0,) * x.ndim)


def context_call(place, lengths, packed, width, kv=None, ctx=None):
    first = kv is None
    rows, n = packed.shape
    heads = (n - (2 * HD if first else 0)) // HD
    args = [lengths, packed]
    specs = [pl.BlockSpec(memory_space=pltpu.SMEM), full(packed)]
    half = jax.ShapeDtypeStruct((rows, HD), BF16)
    context = jax.ShapeDtypeStruct((rows, width), BF16)
    aliases = {}
    if first:
        out_shape = (context, half, half)
        out_specs = (
            pl.BlockSpec((rows, heads * HD), lambda i, place: (0, 0)),
            full(half),
            full(half),
        )
    else:
        args += [kv[0], kv[1], ctx]
        specs += [full(kv[0]), full(kv[1]), pl.BlockSpec(memory_space=pl.ANY)]
        out_shape = context
        out_specs = pl.BlockSpec((rows, heads * HD), lambda i, place: (0, 1))
        aliases = {len(args): 0}
    return pl.pallas_call(
        functools.partial(context_kernel, first, heads),
        out_shape=out_shape,
        grid_spec=pltpu.PrefetchScalarGridSpec(
            num_scalar_prefetch=1,
            grid=(1,),
            in_specs=specs,
            out_specs=out_specs,
            scratch_shapes=[pltpu.VMEM((heads, rows, HD), BF16)],
        ),
        input_output_aliases=aliases,
        cost_estimate=SMALL,
    )(place, *args)


class Order:
    def __init__(self, token):
        self.token = token

    def after(self, x):
        x, self.token = lax.optimization_barrier((x, self.token))
        return x

    note = after


def line_body(tokens, doc_lengths, w_query, w_key, w_value, u_query, u_key, u_value, gammas):
    deep, q_width = w_query.shape
    kv_width = w_key.shape[1]
    widths = (q_width, kv_width, kv_width)
    reps, line, tp_count = lax.axis_size("rep"), lax.axis_size("fsdp"), lax.axis_size("tp")
    rep, slot, place = lax.axis_index("rep"), lax.axis_index("fsdp"), lax.axis_index("tp")
    send = lax.ppermute
    where = jnp.stack([place, rep, slot]).astype(jnp.int32)
    ends, mids, everyone = (0, line - 1), (1, line - 2), tuple(range(line))
    order = Order(doc_lengths)
    after, note = order.after, order.note

    def swap(x, axis, mask, size):
        return send(x, axis, [(i, i ^ mask) for i in range(size)])

    def swap_tp(x, mask, who):
        pairs = [(s * tp_count + i, s * tp_count + (i ^ mask)) for s in who for i in range(tp_count)]
        return send(x, ("fsdp", "tp"), pairs)

    quarter = tokens.shape[0] // tp_count

    def slab(source, mask, out, flips):
        def plan(at):
            return [
                (
                    source,
                    (
                        pl.ds(pl.multiple_of((at[0] ^ flip) * quarter, quarter), quarter),
                        pl.ds(
                            pl.multiple_of(((at[1] ^ r) * line + (at[2] ^ mask)) * deep, deep), deep
                        ),
                    ),
                    out,
                    (pl.ds(j * quarter, quarter), pl.ds(r * deep, deep)),
                )
                for j, flip in enumerate(flips)
                for r in range(reps)
            ]

        return plan

    def piece(rows, columns):
        return jax.ShapeDtypeStruct((rows, columns), BF16)

    def product(x, w):
        return jnp.dot(x[:, :deep], w[0], preferred_element_type=F32) + jnp.dot(
            x[:, deep:], w[1], preferred_element_type=F32
        )

    def arrived(x):
        return note(x)

    def out(x):
        return send(x, "fsdp", [(0, 1), (3, 2)])

    def across(x):
        return send(x, "fsdp", [(1, 2), (2, 1)])

    split = q_width // 2
    wide = 2 * kv_width + split
    total = sum(widths)
    row = jax.ShapeDtypeStruct((1, total), F32)
    lanes = jax.ShapeDtypeStruct((1, 128), F32)

    every = pl.ds(0, deep)
    own_w = [None, None]
    mine, own_w[0] = note(
        gather_blocks(
            where,
            (tokens, w_key, w_value, w_query),
            (piece(quarter, reps * deep), piece(deep, wide)),
            lambda at: slab(0, 3, 0, (0,))(at)
            + [
                (1, (every, pl.ds(0, kv_width)), 1, (every, pl.ds(0, kv_width))),
                (2, (every, pl.ds(0, kv_width)), 1, (every, pl.ds(kv_width, kv_width))),
                (3, (every, pl.ds(0, split)), 1, (every, pl.ds(2 * kv_width, split))),
            ],
        )
    )
    x3e = send(mine, "fsdp", [(0, 3), (3, 0)])
    other_w = [swap(own_w[0], "rep", 1, reps), None]
    x2, x1, x3m, own_w[1] = note(
        gather_blocks(
            after(where),
            (tokens, w_query),
            (
                piece(quarter, reps * deep),
                piece(quarter, reps * deep),
                piece(2 * quarter, reps * deep),
                piece(deep, split),
            ),
            lambda at: slab(0, 2, 0, (0,))(at)
            + slab(0, 1, 1, (0,))(at)
            + slab(0, 3, 2, (0, 2))(at)
            + [(1, (every, pl.ds(split, split)), 3, (every, pl.ds(0, split)))],
        )
    )
    x2 = swap(x2, "fsdp", 2, line)
    x1 = swap(x1, "fsdp", 1, line)
    img = note(
        whole(
            image_kernel,
            jax.ShapeDtypeStruct((3, deep), F32),
            w_query,
            w_key,
            w_value,
            after(u_query[None] + 0.0),
            u_key[None],
            u_value[None],
        )
    )
    img = note(img + swap(img, "tp", 1, tp_count))
    img = note(img + swap(img, "tp", 2, tp_count))
    back = note(
        whole(
            back_kernel,
            jax.ShapeDtypeStruct((1, total + 128), F32),
            w_query,
            w_key,
            w_value,
            img,
        )
    )
    back_x = swap(back, "rep", 1, reps)

    def joint(a, b):
        return note(jnp.concatenate([a, after(b)], axis=0))

    def joined(p, x):
        return note((p + after(x).astype(F32)).astype(HALF))

    x3e = arrived(x3e)
    y3e = swap_tp(x3e, 2, ends)
    rows0 = note(
        gather_blocks(
            after(where),
            (tokens,),
            (piece(tp_count * quarter, reps * deep),),
            slab(0, 0, 0, (0, 2, 1, 3)),
        )[0]
    )
    x2 = arrived(x2)
    y2 = swap_tp(x2, 2, everyone)
    x1 = arrived(x1)
    x3m = across(after(x3m))
    w = [(own_w[0], arrived(other_w[0])), None]
    back = note(back + after(back_x))
    other_w[1] = swap(after(own_w[1]), "rep", 1, reps)
    pair = joint(x3e, y3e)
    c3e = swap_tp(pair, 1, ends)
    back = note(back + after(swap(after(back), "fsdp", 1, line)))
    rows3e = joint(pair, c3e)
    a3 = [out(note(product(after(rows3e), w[0]).astype(HALF))), None]
    y1 = swap_tp(after(x1), 2, everyone)
    p0 = [note(product(after(rows0), w[0])), None]
    pair2 = joint(x2, y2)
    pair1 = joint(x1, y1)
    w[1] = (own_w[1], arrived(other_w[1]))
    a3[1] = out(note(product(after(rows3e), w[1]).astype(HALF)))
    a3[0] = arrived(a3[0])
    x3m = arrived(x3m)
    back_z = swap(after(back), "fsdp", 2, line)
    c2 = swap_tp(after(pair2), 1, everyone)
    c1 = swap_tp(after(pair1), 1, everyone)
    c3m = swap_tp(after(x3m), 1, mids)
    rows2 = joint(pair2, c2)
    p2 = [note(product(after(rows2), w[0])), None]
    v = joined(p2[0], a3[0])
    a2e, a2m = [out(v), None], [across(v), None]
    back = note(back + after(back_z))
    rows1 = joint(pair1, c1)
    rows3m = joint(x3m, c3m)
    p2[1] = note(product(after(rows2), w[1]))
    back, squares = note(whole(functools.partial(length_kernel, widths), (row, lanes), back))
    p3m = [note(product(after(rows3m), w[0])), None]
    a2m[0] = arrived(a2m[0])
    a2e[0] = arrived(a2e[0])
    v = joined(p2[1], a3[1])
    a2e[1], a2m[1] = out(v), across(v)
    a1m = [across(joined(p3m[0], a2e[0])), None]
    p1 = [note(product(after(rows1), w[0])), None]
    a1p = [swap(joined(p1[0], a2m[0]), "fsdp", 1, line), None]
    squares = note(squares + after(swap(after(squares), "tp", 1, tp_count)))
    squares = note(squares + after(swap(squares, "tp", 2, tp_count)))
    a2m[1] = arrived(a2m[1])
    a2e[1] = arrived(a2e[1])
    p1[1] = note(product(after(rows1), w[1]))
    a1p[1] = swap(joined(p1[1], a2m[1]), "fsdp", 1, line)
    p3m[1] = note(product(after(rows3m), w[1]))
    a1m[1] = across(joined(p3m[1], a2e[1]))
    p0[1] = note(product(after(rows0), w[1]))
    states = note(
        whole(
            functools.partial(state_kernel, widths, tp_count),
            tuple(jax.ShapeDtypeStruct((1, n), F32) for n in widths) + (lanes, row),
            back,
            after(squares),
            gammas,
        )
    )
    factors = states[4]
    factor = [factors[:, :wide], factors[:, wide:]]

    def packed(c):
        near, far = after((a1p[c], a1m[c]))
        return note((factor[c] * (p0[c] + near.astype(F32) + far.astype(F32))).astype(BF16))

    first = packed(0)
    ctx, keys, values = note(context_call(where, order.token, first, q_width))
    second = packed(1)
    context = context_call(where, order.token, second, q_width, (keys, values), ctx)
    return (context, states[0][0], states[1][0], states[2][0], states[3][0, :3])


def solution(mesh):
    in_specs = (
        P(("rep", "fsdp"), None),
        P(("rep", "fsdp"), None),
        P(("rep", "fsdp"), "tp"),
        P(("rep", "fsdp"), "tp"),
        P(("rep", "fsdp"), "tp"),
        P("tp"),
        P("tp"),
        P("tp"),
        P(),
    )
    out_specs = (P(("rep", "fsdp"), "tp"), P("tp"), P("tp"), P("tp"), P())
    sizes = tuple(mesh.shape[name] for name in ("rep", "fsdp", "tp"))
    body = line_body if sizes == (2, 4, 4) else gather_body
    return jax.shard_map(body, mesh=mesh, in_specs=in_specs, out_specs=out_specs, check_vma=False)
```

```python
import functools

import jax
import jax.numpy as jnp
from jax import lax
from jax.experimental import pallas as pl
from jax.experimental.pallas import tpu as pltpu
from jax.sharding import PartitionSpec as P

HEADS = 32
KV_HEADS = 4
HD = 128
DOC_MOST = 192

EPSILON = 1e-12
HIGHEST = lax.Precision.HIGHEST
MASKED = -1e30
ROWS = ("rep", "fsdp")
F32 = jnp.float32
SMALL = pl.CostEstimate(flops=1, bytes_accessed=1, transcendentals=0)
BF16 = jnp.bfloat16
HALF = jnp.float16


def attention(queries, key_heads, value_heads, lengths):
    tok_rows = queries.shape[0]
    scores = jnp.einsum(
        "tkgd,skd->kgts", queries, key_heads, preferred_element_type=F32
    ) * queries.shape[-1] ** (-0.5)
    doc_ends = jnp.cumsum(lengths)
    position = jnp.arange(tok_rows, dtype=jnp.int32)
    doc_ids = jnp.sum((position[:, None] >= doc_ends[None, :]).astype(jnp.int32), axis=1)
    allowed = (doc_ids[:, None] == doc_ids[None, :]) & (position[None, :] <= position[:, None])
    scores = jnp.where(allowed, scores, MASKED)
    row_max = jnp.max(scores, axis=-1, keepdims=True)
    exponent = jnp.exp(scores - row_max)
    attn_probs = (exponent / jnp.sum(exponent, axis=-1, keepdims=True)).astype(BF16)
    mixed = jnp.einsum("kgts,skd->tkgd", attn_probs, value_heads, preferred_element_type=F32)
    return mixed.astype(BF16).reshape(tok_rows, -1)


def gather_body(tokens, doc_lengths, w_query, w_key, w_value, u_query, u_key, u_value, gammas):
    tok_rows = tokens.shape[0]
    widened = [w_query.astype(F32), w_key.astype(F32), w_value.astype(F32)]
    local_images = [
        jnp.dot(matrix, vector, precision=HIGHEST)
        for matrix, vector in zip(widened, (u_query, u_key, u_value))
    ]
    images = lax.psum((local_images[0], local_images[1], local_images[2]), "tp")
    squares = [jnp.sum(image * image) for image in images]
    norms = lax.psum((squares[0], squares[1], squares[2]), ROWS)
    partial_backs = [
        jnp.dot(image * lax.rsqrt(total_sq + EPSILON), matrix, precision=HIGHEST)
        for image, total_sq, matrix in zip(images, norms, widened)
    ]
    backs = lax.psum((partial_backs[0], partial_backs[1], partial_backs[2]), ROWS)
    back_sq = lax.psum(tuple(jnp.sum(back * back) for back in backs), "tp")
    sigma_list = [jnp.sqrt(total_sq + EPSILON) for total_sq in back_sq]
    tp_count = lax.axis_size("tp")
    new_states = [
        backed * (jnp.sqrt(F32(backed.shape[0] * tp_count)) / sigma)
        for backed, sigma in zip(backs, sigma_list)
    ]
    sigmas = jnp.stack(sigma_list)
    products = [
        jnp.dot(
            tokens, lax.all_gather(w, ROWS, axis=0, tiled=True), preferred_element_type=F32
        )
        for w in (w_query, w_key, w_value)
    ]
    scales = gammas / sigmas
    scaled = [(scales[which] * products[which]).astype(BF16) for which in range(3)]
    per_group = HEADS // KV_HEADS
    queries = scaled[0].reshape(tok_rows, -1, per_group, HD)
    key_heads = scaled[1].reshape(tok_rows, -1, HD)
    value_heads = scaled[2].reshape(tok_rows, -1, HD)
    context = attention(queries, key_heads, value_heads, doc_lengths[0])
    return (context, new_states[0], new_states[1], new_states[2], sigmas)


def stacked_terms(row):
    high = row.astype(BF16).astype(F32)
    rest = row - high
    middle = rest.astype(BF16).astype(F32)
    low = rest - middle
    which = lax.broadcasted_iota(jnp.int32, (8, row.shape[1]), 0)
    zero = jnp.zeros((8, row.shape[1]), F32)
    out = jnp.where(which == 0, high, jnp.where(which == 1, middle, jnp.where(which == 2, low, zero)))
    return out.astype(BF16)


def image_kernel(wq, wk, wv, uq, uk, uv, out):
    for i, (w, u) in enumerate(((wq, uq), (wk, uk), (wv, uv))):
        terms = lax.dot_general(
            stacked_terms(u[...]), w[...], (((1,), (1,)), ((), ())), preferred_element_type=F32
        )
        out[i : i + 1, :] = jnp.sum(terms, axis=0, keepdims=True)


def back_kernel(wq, wk, wv, image, out):
    lane = lax.broadcasted_iota(jnp.int32, (1, 128), 1)
    norms = jnp.zeros((1, 128), F32)
    at = 0
    for i, w in enumerate((wq, wk, wv)):
        row = image[i : i + 1, :]
        terms = jnp.dot(stacked_terms(row), w[...], preferred_element_type=F32)
        out[:, at : at + w.shape[1]] = jnp.sum(terms, axis=0, keepdims=True)
        at += w.shape[1]
        norms = jnp.where(lane == i, jnp.sum(row * row, axis=1, keepdims=True), norms)
    out[:, at : at + 128] = norms


def length_kernel(widths, summed, back, squares):
    lane = lax.broadcasted_iota(jnp.int32, (1, 128), 1)
    total = sum(widths)
    found = jnp.zeros((1, 128), F32)
    at = 0
    for i, width in enumerate(widths):
        norm = summed[:, total + i : total + i + 1]
        row = summed[:, at : at + width] * lax.rsqrt(norm + EPSILON)
        back[:, at : at + width] = row
        found = jnp.where(lane == i, jnp.sum(row * row, axis=1, keepdims=True), found)
        at += width
    squares[...] = found


def state_kernel(widths, tp_count, back, squares, gammas, new_q, new_k, new_v, sigmas, factors):
    sigma = jnp.sqrt(squares[...] + EPSILON)
    sigmas[...] = sigma
    for i, (start, width) in enumerate(
        ((2 * widths[1], widths[0]), (0, widths[1]), (widths[1], widths[2]))
    ):
        factors[:, start : start + width] = jnp.broadcast_to(
            gammas[i] / sigma[:, i : i + 1], (1, width)
        )
    at = 0
    for i, (width, out) in enumerate(zip(widths, (new_q, new_k, new_v))):
        factor = jnp.sqrt(jnp.full((1, 1), width * tp_count, F32)) / sigma[:, i : i + 1]
        out[...] = back[:, at : at + width] * factor
        at += width


def whole(kernel, out_shape, *args):
    specs = [
        pl.BlockSpec(memory_space=pltpu.SMEM if a.ndim == 1 else pltpu.VMEM) for a in args
    ]
    return pl.pallas_call(kernel, out_shape=out_shape, in_specs=specs, cost_estimate=SMALL)(*args)


def gather_blocks(where, sources, outs, plan):
    count = len(plan([0, 0, 0]))
    n = len(sources)

    def kernel(where_ref, *refs):
        sems = refs[-1]
        place = [where_ref[i] for i in range(3)]
        copies = [
            pltpu.make_async_copy(refs[s].at[at], refs[n + o].at[to], sems.at[i])
            for i, (s, at, o, to) in enumerate(plan(place))
        ]
        for copy in copies:
            copy.start()
        for copy in copies:
            copy.wait()

    anywhere = pl.BlockSpec(memory_space=pl.ANY)
    return pl.pallas_call(
        kernel,
        out_shape=outs,
        grid_spec=pltpu.PrefetchScalarGridSpec(
            num_scalar_prefetch=1,
            grid=(1,),
            in_specs=[anywhere] * n,
            out_specs=tuple(pl.BlockSpec(o.shape, lambda i, where: (0, 0)) for o in outs),
            scratch_shapes=[pltpu.SemaphoreType.DMA((count,))],
        ),
        cost_estimate=SMALL,
    )(where, *sources)


def context_kernel(first, heads, place, lengths, packed, *refs):
    if first:
        ctx, keys, values, scaled = refs
    else:
        keys, values, _, ctx, scaled = refs
    rows = packed.shape[0]
    block = rows // 4
    at = 2 * HD if first else 0
    for i, j in enumerate((0, 2, 1, 3)):
        here = pl.ds(i * block, block)
        there = pl.ds(pl.multiple_of((place[0] ^ j) * block, block), block)
        if first:
            keys[there, :] = packed[here, :HD]
            values[there, :] = packed[here, HD:at]
        for h in range(heads):
            scaled[h, there, :] = packed[here, at + h * HD : at + (h + 1) * HD]
    for i in range(rows // block):
        low = max(0, (i * block - DOC_MOST + 1) // HD * HD)
        high = (i + 1) * block
        position = lax.broadcasted_iota(jnp.int32, (block, 1), 0) + i * block
        start = jnp.zeros((block, 1), jnp.int32)
        end = 0
        for k in range(lengths.shape[1]):
            end = end + lengths[0, k]
            start = jnp.where(position >= end, end, start)
        key_at = lax.broadcasted_iota(jnp.int32, (block, high - low), 1) + low
        allowed = ((key_at >= start) & (key_at <= position))[None]
        q = scaled[:, i * block : high, :].reshape(heads * block, HD)
        s = lax.dot_general(
            q, keys[low:high, :], (((1,), (1,)), ((), ())), preferred_element_type=F32
        ).reshape(heads, block, high - low)
        s = jnp.where(allowed, s * HD ** (-0.5), MASKED)
        e = jnp.exp(s - jnp.max(s, axis=2, keepdims=True))
        p = (e * (1.0 / jnp.sum(e, axis=2, keepdims=True))).astype(BF16)
        mixed = jnp.dot(
            p.reshape(heads * block, high - low), values[low:high, :], preferred_element_type=F32
        ).astype(BF16)
        for h in range(heads):
            ctx[i * block : high, h * HD : (h + 1) * HD] = mixed[h * block : (h + 1) * block, :]


def full(x):
    return pl.BlockSpec(x.shape, lambda i, place: (0,) * x.ndim)


def context_call(place, lengths, packed, width, kv=None, ctx=None):
    first = kv is None
    rows, n = packed.shape
    heads = (n - (2 * HD if first else 0)) // HD
    args = [lengths, packed]
    specs = [pl.BlockSpec(memory_space=pltpu.SMEM), full(packed)]
    half = jax.ShapeDtypeStruct((rows, HD), BF16)
    context = jax.ShapeDtypeStruct((rows, width), BF16)
    aliases = {}
    if first:
        out_shape = (context, half, half)
        out_specs = (
            pl.BlockSpec((rows, heads * HD), lambda i, place: (0, 0)),
            full(half),
            full(half),
        )
    else:
        args += [kv[0], kv[1], ctx]
        specs += [full(kv[0]), full(kv[1]), pl.BlockSpec(memory_space=pl.ANY)]
        out_shape = context
        out_specs = pl.BlockSpec((rows, heads * HD), lambda i, place: (0, 1))
        aliases = {len(args): 0}
    return pl.pallas_call(
        functools.partial(context_kernel, first, heads),
        out_shape=out_shape,
        grid_spec=pltpu.PrefetchScalarGridSpec(
            num_scalar_prefetch=1,
            grid=(1,),
            in_specs=specs,
            out_specs=out_specs,
            scratch_shapes=[pltpu.VMEM((heads, rows, HD), BF16)],
        ),
        input_output_aliases=aliases,
        cost_estimate=SMALL,
    )(place, *args)


class Order:
    def __init__(self, token):
        self.token = token

    def after(self, x):
        x, self.token = lax.optimization_barrier((x, self.token))
        return x

    note = after


def line_body(tokens, doc_lengths, w_query, w_key, w_value, u_query, u_key, u_value, gammas):
    deep, q_width = w_query.shape
    kv_width = w_key.shape[1]
    widths = (q_width, kv_width, kv_width)
    reps, line, tp_count = lax.axis_size("rep"), lax.axis_size("fsdp"), lax.axis_size("tp")
    rep, slot, place = lax.axis_index("rep"), lax.axis_index("fsdp"), lax.axis_index("tp")
    send = lax.ppermute
    where = jnp.stack([place, rep, slot]).astype(jnp.int32)
    ends, mids, everyone = (0, line - 1), (1, line - 2), tuple(range(line))
    order = Order(doc_lengths)
    after, note = order.after, order.note

    def swap(x, axis, mask, size):
        return send(x, axis, [(i, i ^ mask) for i in range(size)])

    def swap_tp(x, mask, who):
        pairs = [(s * tp_count + i, s * tp_count + (i ^ mask)) for s in who for i in range(tp_count)]
        return send(x, ("fsdp", "tp"), pairs)

    quarter = tokens.shape[0] // tp_count

    def slab(source, mask, out, flips):
        def plan(at):
            return [
                (
                    source,
                    (
                        pl.ds(pl.multiple_of((at[0] ^ flip) * quarter, quarter), quarter),
                        pl.ds(
                            pl.multiple_of(((at[1] ^ r) * line + (at[2] ^ mask)) * deep, deep), deep
                        ),
                    ),
                    out,
                    (pl.ds(j * quarter, quarter), pl.ds(r * deep, deep)),
                )
                for j, flip in enumerate(flips)
                for r in range(reps)
            ]

        return plan

    def piece(rows, columns):
        return jax.ShapeDtypeStruct((rows, columns), BF16)

    def product(x, w):
        return jnp.dot(x[:, :deep], w[0], preferred_element_type=F32) + jnp.dot(
            x[:, deep:], w[1], preferred_element_type=F32
        )

    def arrived(x):
        return note(x)

    def out(x):
        return send(x, "fsdp", [(0, 1), (3, 2)])

    def across(x):
        return send(x, "fsdp", [(1, 2), (2, 1)])

    split = q_width // 2
    wide = 2 * kv_width + split
    total = sum(widths)
    row = jax.ShapeDtypeStruct((1, total), F32)
    lanes = jax.ShapeDtypeStruct((1, 128), F32)

    every = pl.ds(0, deep)
    own_w = [None, None]
    mine, own_w[0] = note(
        gather_blocks(
            where,
            (tokens, w_key, w_value, w_query),
            (piece(quarter, reps * deep), piece(deep, wide)),
            lambda at: slab(0, 3, 0, (0,))(at)
            + [
                (1, (every, pl.ds(0, kv_width)), 1, (every, pl.ds(0, kv_width))),
                (2, (every, pl.ds(0, kv_width)), 1, (every, pl.ds(kv_width, kv_width))),
                (3, (every, pl.ds(0, split)), 1, (every, pl.ds(2 * kv_width, split))),
            ],
        )
    )
    x3e = send(mine, "fsdp", [(0, 3), (3, 0)])
    other_w = [swap(own_w[0], "rep", 1, reps), None]
    x2, x1, x3m, own_w[1] = note(
        gather_blocks(
            after(where),
            (tokens, w_query),
            (
                piece(quarter, reps * deep),
                piece(quarter, reps * deep),
                piece(2 * quarter, reps * deep),
                piece(deep, split),
            ),
            lambda at: slab(0, 2, 0, (0,))(at)
            + slab(0, 1, 1, (0,))(at)
            + slab(0, 3, 2, (0, 2))(at)
            + [(1, (every, pl.ds(split, split)), 3, (every, pl.ds(0, split)))],
        )
    )
    x2 = swap(x2, "fsdp", 2, line)
    x1 = swap(x1, "fsdp", 1, line)
    img = note(
        whole(
            image_kernel,
            jax.ShapeDtypeStruct((3, deep), F32),
            w_query,
            w_key,
            w_value,
            after(u_query[None] + 0.0),
            u_key[None],
            u_value[None],
        )
    )
    img = note(img + swap(img, "tp", 1, tp_count))
    img = note(img + swap(img, "tp", 2, tp_count))
    back = note(
        whole(
            back_kernel,
            jax.ShapeDtypeStruct((1, total + 128), F32),
            w_query,
            w_key,
            w_value,
            img,
        )
    )
    back_x = swap(back, "rep", 1, reps)

    def joint(a, b):
        return note(jnp.concatenate([a, after(b)], axis=0))

    def joined(p, x):
        return note((p + after(x).astype(F32)).astype(HALF))

    x3e = arrived(x3e)
    y3e = swap_tp(x3e, 2, ends)
    rows0 = note(
        gather_blocks(
            after(where),
            (tokens,),
            (piece(tp_count * quarter, reps * deep),),
            slab(0, 0, 0, (0, 2, 1, 3)),
        )[0]
    )
    x2 = arrived(x2)
    y2 = swap_tp(x2, 2, everyone)
    x1 = arrived(x1)
    x3m = across(after(x3m))
    w = [(own_w[0], arrived(other_w[0])), None]
    back = note(back + after(back_x))
    other_w[1] = swap(after(own_w[1]), "rep", 1, reps)
    pair = joint(x3e, y3e)
    c3e = swap_tp(pair, 1, ends)
    back = note(back + after(swap(after(back), "fsdp", 1, line)))
    rows3e = joint(pair, c3e)
    a3 = [out(note(product(after(rows3e), w[0]).astype(HALF))), None]
    y1 = swap_tp(after(x1), 2, everyone)
    pair1 = joint(x1, y1)
    pair2 = joint(x2, y2)
    w[1] = (own_w[1], arrived(other_w[1]))
    a3[1] = out(note(product(after(rows3e), w[1]).astype(HALF)))
    a3[0] = arrived(a3[0])
    x3m = arrived(x3m)
    back_z = swap(after(back), "fsdp", 2, line)
    c2 = swap_tp(after(pair2), 1, everyone)
    c1 = swap_tp(after(pair1), 1, everyone)
    c3m = swap_tp(after(x3m), 1, mids)
    rows2 = joint(pair2, c2)
    p2 = [note(product(after(rows2), w[0])), None]
    v = joined(p2[0], a3[0])
    a2e, a2m = [out(v), None], [across(v), None]
    back = note(back + after(back_z))
    rows1 = joint(pair1, c1)
    rows3m = joint(x3m, c3m)
    p2[1] = note(product(after(rows2), w[1]))
    back, squares = note(whole(functools.partial(length_kernel, widths), (row, lanes), back))
    p3m = [note(product(after(rows3m), w[0])), None]
    a2m[0] = arrived(a2m[0])
    a2e[0] = arrived(a2e[0])
    v = joined(p2[1], a3[1])
    a2e[1], a2m[1] = out(v), across(v)
    a1m = [across(joined(p3m[0], a2e[0])), None]
    p1 = [note(product(after(rows1), w[0])), None]
    a1p = [swap(joined(p1[0], a2m[0]), "fsdp", 1, line), None]
    squares = note(squares + after(swap(after(squares), "tp", 1, tp_count)))
    squares = note(squares + after(swap(squares, "tp", 2, tp_count)))
    a2m[1] = arrived(a2m[1])
    a2e[1] = arrived(a2e[1])
    p1[1] = note(product(after(rows1), w[1]))
    a1p[1] = swap(joined(p1[1], a2m[1]), "fsdp", 1, line)
    p3m[1] = note(product(after(rows3m), w[1]))
    a1m[1] = across(joined(p3m[1], a2e[1]))
    p0 = [note(product(after(rows0), w[c])) for c in range(2)]
    states = note(
        whole(
            functools.partial(state_kernel, widths, tp_count),
            tuple(jax.ShapeDtypeStruct((1, n), F32) for n in widths) + (lanes, row),
            back,
            after(squares),
            gammas,
        )
    )
    factors = states[4]
    factor = [factors[:, :wide], factors[:, wide:]]

    def packed(c):
        near, far = after((a1p[c], a1m[c]))
        return note((factor[c] * (p0[c] + near.astype(F32) + far.astype(F32))).astype(BF16))

    first = packed(0)
    ctx, keys, values = note(context_call(where, order.token, first, q_width))
    second = packed(1)
    context = context_call(where, order.token, second, q_width, (keys, values), ctx)
    return (context, states[0][0], states[1][0], states[2][0], states[3][0, :3])


def solution(mesh):
    in_specs = (
        P(("rep", "fsdp"), None),
        P(("rep", "fsdp"), None),
        P(("rep", "fsdp"), "tp"),
        P(("rep", "fsdp"), "tp"),
        P(("rep", "fsdp"), "tp"),
        P("tp"),
        P("tp"),
        P("tp"),
        P(),
    )
    out_specs = (P(("rep", "fsdp"), "tp"), P("tp"), P("tp"), P("tp"), P())
    sizes = tuple(mesh.shape[name] for name in ("rep", "fsdp", "tp"))
    body = line_body if sizes == (2, 4, 4) else gather_body
    return jax.shard_map(body, mesh=mesh, in_specs=in_specs, out_specs=out_specs, check_vma=False)
```

```python
import functools

import jax
import jax.numpy as jnp
from jax import lax
from jax.experimental import pallas as pl
from jax.experimental.pallas import tpu as pltpu
from jax.sharding import PartitionSpec as P

HEADS = 32
KV_HEADS = 4
HD = 128
DOC_MOST = 192

EPSILON = 1e-12
HIGHEST = lax.Precision.HIGHEST
MASKED = -1e30
ROWS = ("rep", "fsdp")
F32 = jnp.float32
SMALL = pl.CostEstimate(flops=1, bytes_accessed=1, transcendentals=0)
BF16 = jnp.bfloat16
HALF = jnp.float16


def attention(queries, key_heads, value_heads, lengths):
    tok_rows = queries.shape[0]
    scores = jnp.einsum(
        "tkgd,skd->kgts", queries, key_heads, preferred_element_type=F32
    ) * queries.shape[-1] ** (-0.5)
    doc_ends = jnp.cumsum(lengths)
    position = jnp.arange(tok_rows, dtype=jnp.int32)
    doc_ids = jnp.sum((position[:, None] >= doc_ends[None, :]).astype(jnp.int32), axis=1)
    allowed = (doc_ids[:, None] == doc_ids[None, :]) & (position[None, :] <= position[:, None])
    scores = jnp.where(allowed, scores, MASKED)
    row_max = jnp.max(scores, axis=-1, keepdims=True)
    exponent = jnp.exp(scores - row_max)
    attn_probs = (exponent / jnp.sum(exponent, axis=-1, keepdims=True)).astype(BF16)
    mixed = jnp.einsum("kgts,skd->tkgd", attn_probs, value_heads, preferred_element_type=F32)
    return mixed.astype(BF16).reshape(tok_rows, -1)


def gather_body(tokens, doc_lengths, w_query, w_key, w_value, u_query, u_key, u_value, gammas):
    tok_rows = tokens.shape[0]
    widened = [w_query.astype(F32), w_key.astype(F32), w_value.astype(F32)]
    local_images = [
        jnp.dot(matrix, vector, precision=HIGHEST)
        for matrix, vector in zip(widened, (u_query, u_key, u_value))
    ]
    images = lax.psum((local_images[0], local_images[1], local_images[2]), "tp")
    squares = [jnp.sum(image * image) for image in images]
    norms = lax.psum((squares[0], squares[1], squares[2]), ROWS)
    partial_backs = [
        jnp.dot(image * lax.rsqrt(total_sq + EPSILON), matrix, precision=HIGHEST)
        for image, total_sq, matrix in zip(images, norms, widened)
    ]
    backs = lax.psum((partial_backs[0], partial_backs[1], partial_backs[2]), ROWS)
    back_sq = lax.psum(tuple(jnp.sum(back * back) for back in backs), "tp")
    sigma_list = [jnp.sqrt(total_sq + EPSILON) for total_sq in back_sq]
    tp_count = lax.axis_size("tp")
    new_states = [
        backed * (jnp.sqrt(F32(backed.shape[0] * tp_count)) / sigma)
        for backed, sigma in zip(backs, sigma_list)
    ]
    sigmas = jnp.stack(sigma_list)
    products = [
        jnp.dot(
            tokens, lax.all_gather(w, ROWS, axis=0, tiled=True), preferred_element_type=F32
        )
        for w in (w_query, w_key, w_value)
    ]
    scales = gammas / sigmas
    scaled = [(scales[which] * products[which]).astype(BF16) for which in range(3)]
    per_group = HEADS // KV_HEADS
    queries = scaled[0].reshape(tok_rows, -1, per_group, HD)
    key_heads = scaled[1].reshape(tok_rows, -1, HD)
    value_heads = scaled[2].reshape(tok_rows, -1, HD)
    context = attention(queries, key_heads, value_heads, doc_lengths[0])
    return (context, new_states[0], new_states[1], new_states[2], sigmas)


def stacked_terms(row):
    high = row.astype(BF16).astype(F32)
    rest = row - high
    middle = rest.astype(BF16).astype(F32)
    low = rest - middle
    which = lax.broadcasted_iota(jnp.int32, (8, row.shape[1]), 0)
    zero = jnp.zeros((8, row.shape[1]), F32)
    out = jnp.where(which == 0, high, jnp.where(which == 1, middle, jnp.where(which == 2, low, zero)))
    return out.astype(BF16)


def image_kernel(wq, wk, wv, uq, uk, uv, out):
    for i, (w, u) in enumerate(((wq, uq), (wk, uk), (wv, uv))):
        terms = lax.dot_general(
            stacked_terms(u[...]), w[...], (((1,), (1,)), ((), ())), preferred_element_type=F32
        )
        out[i : i + 1, :] = jnp.sum(terms, axis=0, keepdims=True)


def back_kernel(wq, wk, wv, image, out):
    lane = lax.broadcasted_iota(jnp.int32, (1, 128), 1)
    norms = jnp.zeros((1, 128), F32)
    at = 0
    for i, w in enumerate((wq, wk, wv)):
        row = image[i : i + 1, :]
        terms = jnp.dot(stacked_terms(row), w[...], preferred_element_type=F32)
        out[:, at : at + w.shape[1]] = jnp.sum(terms, axis=0, keepdims=True)
        at += w.shape[1]
        norms = jnp.where(lane == i, jnp.sum(row * row, axis=1, keepdims=True), norms)
    out[:, at : at + 128] = norms


def length_kernel(widths, summed, back, squares):
    lane = lax.broadcasted_iota(jnp.int32, (1, 128), 1)
    total = sum(widths)
    found = jnp.zeros((1, 128), F32)
    at = 0
    for i, width in enumerate(widths):
        norm = summed[:, total + i : total + i + 1]
        row = summed[:, at : at + width] * lax.rsqrt(norm + EPSILON)
        back[:, at : at + width] = row
        found = jnp.where(lane == i, jnp.sum(row * row, axis=1, keepdims=True), found)
        at += width
    squares[...] = found


def state_kernel(widths, tp_count, back, squares, gammas, new_q, new_k, new_v, sigmas, factors):
    sigma = jnp.sqrt(squares[...] + EPSILON)
    sigmas[...] = sigma
    for i, (start, width) in enumerate(
        ((2 * widths[1], widths[0]), (0, widths[1]), (widths[1], widths[2]))
    ):
        factors[:, start : start + width] = jnp.broadcast_to(
            gammas[i] / sigma[:, i : i + 1], (1, width)
        )
    at = 0
    for i, (width, out) in enumerate(zip(widths, (new_q, new_k, new_v))):
        factor = jnp.sqrt(jnp.full((1, 1), width * tp_count, F32)) / sigma[:, i : i + 1]
        out[...] = back[:, at : at + width] * factor
        at += width


def whole(kernel, out_shape, *args):
    specs = [
        pl.BlockSpec(memory_space=pltpu.SMEM if a.ndim == 1 else pltpu.VMEM) for a in args
    ]
    return pl.pallas_call(kernel, out_shape=out_shape, in_specs=specs, cost_estimate=SMALL)(*args)


def gather_blocks(where, sources, outs, plan):
    count = len(plan([0, 0, 0]))
    n = len(sources)

    def kernel(where_ref, *refs):
        sems = refs[-1]
        place = [where_ref[i] for i in range(3)]
        copies = [
            pltpu.make_async_copy(refs[s].at[at], refs[n + o].at[to], sems.at[i])
            for i, (s, at, o, to) in enumerate(plan(place))
        ]
        for copy in copies:
            copy.start()
        for copy in copies:
            copy.wait()

    anywhere = pl.BlockSpec(memory_space=pl.ANY)
    return pl.pallas_call(
        kernel,
        out_shape=outs,
        grid_spec=pltpu.PrefetchScalarGridSpec(
            num_scalar_prefetch=1,
            grid=(1,),
            in_specs=[anywhere] * n,
            out_specs=tuple(pl.BlockSpec(o.shape, lambda i, where: (0, 0)) for o in outs),
            scratch_shapes=[pltpu.SemaphoreType.DMA((count,))],
        ),
        cost_estimate=SMALL,
    )(where, *sources)


def context_kernel(first, heads, place, lengths, packed, *refs):
    if first:
        ctx, keys, values, scaled = refs
    else:
        keys, values, _, ctx, scaled = refs
    rows = packed.shape[0]
    block = rows // 4
    at = 2 * HD if first else 0
    for i, j in enumerate((0, 2, 1, 3)):
        here = pl.ds(i * block, block)
        there = pl.ds(pl.multiple_of((place[0] ^ j) * block, block), block)
        if first:
            keys[there, :] = packed[here, :HD]
            values[there, :] = packed[here, HD:at]
        for h in range(heads):
            scaled[h, there, :] = packed[here, at + h * HD : at + (h + 1) * HD]
    for i in range(rows // block):
        low = max(0, (i * block - DOC_MOST + 1) // HD * HD)
        high = (i + 1) * block
        position = lax.broadcasted_iota(jnp.int32, (block, 1), 0) + i * block
        start = jnp.zeros((block, 1), jnp.int32)
        end = 0
        for k in range(lengths.shape[1]):
            end = end + lengths[0, k]
            start = jnp.where(position >= end, end, start)
        key_at = lax.broadcasted_iota(jnp.int32, (block, high - low), 1) + low
        allowed = ((key_at >= start) & (key_at <= position))[None]
        q = scaled[:, i * block : high, :].reshape(heads * block, HD)
        s = lax.dot_general(
            q, keys[low:high, :], (((1,), (1,)), ((), ())), preferred_element_type=F32
        ).reshape(heads, block, high - low)
        s = jnp.where(allowed, s * HD ** (-0.5), MASKED)
        e = jnp.exp(s - jnp.max(s, axis=2, keepdims=True))
        total = jnp.sum(e, axis=2, keepdims=True).reshape(heads * block, 1)
        p = e.astype(BF16).reshape(heads * block, high - low)
        mixed = jnp.dot(p, values[low:high, :], preferred_element_type=F32)
        mixed = (mixed * (1.0 / total)).astype(BF16)
        for h in range(heads):
            ctx[i * block : high, h * HD : (h + 1) * HD] = mixed[h * block : (h + 1) * block, :]


def full(x):
    return pl.BlockSpec(x.shape, lambda i, place: (0,) * x.ndim)


def context_call(place, lengths, packed, width, kv=None, ctx=None):
    first = kv is None
    rows, n = packed.shape
    heads = (n - (2 * HD if first else 0)) // HD
    args = [lengths, packed]
    specs = [pl.BlockSpec(memory_space=pltpu.SMEM), full(packed)]
    half = jax.ShapeDtypeStruct((rows, HD), BF16)
    context = jax.ShapeDtypeStruct((rows, width), BF16)
    aliases = {}
    if first:
        out_shape = (context, half, half)
        out_specs = (
            pl.BlockSpec((rows, heads * HD), lambda i, place: (0, 0)),
            full(half),
            full(half),
        )
    else:
        args += [kv[0], kv[1], ctx]
        specs += [full(kv[0]), full(kv[1]), pl.BlockSpec(memory_space=pl.ANY)]
        out_shape = context
        out_specs = pl.BlockSpec((rows, heads * HD), lambda i, place: (0, 1))
        aliases = {len(args): 0}
    return pl.pallas_call(
        functools.partial(context_kernel, first, heads),
        out_shape=out_shape,
        grid_spec=pltpu.PrefetchScalarGridSpec(
            num_scalar_prefetch=1,
            grid=(1,),
            in_specs=specs,
            out_specs=out_specs,
            scratch_shapes=[pltpu.VMEM((heads, rows, HD), BF16)],
        ),
        input_output_aliases=aliases,
        cost_estimate=SMALL,
    )(place, *args)


class Order:
    def __init__(self, token):
        self.token = token

    def after(self, x):
        x, self.token = lax.optimization_barrier((x, self.token))
        return x

    note = after


def line_body(tokens, doc_lengths, w_query, w_key, w_value, u_query, u_key, u_value, gammas):
    deep, q_width = w_query.shape
    kv_width = w_key.shape[1]
    widths = (q_width, kv_width, kv_width)
    reps, line, tp_count = lax.axis_size("rep"), lax.axis_size("fsdp"), lax.axis_size("tp")
    rep, slot, place = lax.axis_index("rep"), lax.axis_index("fsdp"), lax.axis_index("tp")
    send = lax.ppermute
    where = jnp.stack([place, rep, slot]).astype(jnp.int32)
    ends, mids, everyone = (0, line - 1), (1, line - 2), tuple(range(line))
    order = Order(doc_lengths)
    after, note = order.after, order.note

    def swap(x, axis, mask, size):
        return send(x, axis, [(i, i ^ mask) for i in range(size)])

    def swap_tp(x, mask, who):
        pairs = [(s * tp_count + i, s * tp_count + (i ^ mask)) for s in who for i in range(tp_count)]
        return send(x, ("fsdp", "tp"), pairs)

    quarter = tokens.shape[0] // tp_count

    def slab(source, mask, out, flips):
        def plan(at):
            return [
                (
                    source,
                    (
                        pl.ds(pl.multiple_of((at[0] ^ flip) * quarter, quarter), quarter),
                        pl.ds(
                            pl.multiple_of(((at[1] ^ r) * line + (at[2] ^ mask)) * deep, deep), deep
                        ),
                    ),
                    out,
                    (pl.ds(j * quarter, quarter), pl.ds(r * deep, deep)),
                )
                for j, flip in enumerate(flips)
                for r in range(reps)
            ]

        return plan

    def piece(rows, columns):
        return jax.ShapeDtypeStruct((rows, columns), BF16)

    def product(x, w):
        return jnp.dot(x[:, :deep], w[0], preferred_element_type=F32) + jnp.dot(
            x[:, deep:], w[1], preferred_element_type=F32
        )

    def arrived(x):
        return note(x)

    def out(x):
        return send(x, "fsdp", [(0, 1), (3, 2)])

    def across(x):
        return send(x, "fsdp", [(1, 2), (2, 1)])

    split = q_width // 2
    wide = 2 * kv_width + split
    total = sum(widths)
    row = jax.ShapeDtypeStruct((1, total), F32)
    lanes = jax.ShapeDtypeStruct((1, 128), F32)

    every = pl.ds(0, deep)
    own_w = [None, None]
    mine, own_w[0] = note(
        gather_blocks(
            where,
            (tokens, w_key, w_value, w_query),
            (piece(quarter, reps * deep), piece(deep, wide)),
            lambda at: slab(0, 3, 0, (0,))(at)
            + [
                (1, (every, pl.ds(0, kv_width)), 1, (every, pl.ds(0, kv_width))),
                (2, (every, pl.ds(0, kv_width)), 1, (every, pl.ds(kv_width, kv_width))),
                (3, (every, pl.ds(0, split)), 1, (every, pl.ds(2 * kv_width, split))),
            ],
        )
    )
    x3e = send(mine, "fsdp", [(0, 3), (3, 0)])
    other_w = [swap(own_w[0], "rep", 1, reps), None]
    x2, x1, x3m, own_w[1] = note(
        gather_blocks(
            after(where),
            (tokens, w_query),
            (
                piece(quarter, reps * deep),
                piece(quarter, reps * deep),
                piece(2 * quarter, reps * deep),
                piece(deep, split),
            ),
            lambda at: slab(0, 2, 0, (0,))(at)
            + slab(0, 1, 1, (0,))(at)
            + slab(0, 3, 2, (0, 2))(at)
            + [(1, (every, pl.ds(split, split)), 3, (every, pl.ds(0, split)))],
        )
    )
    x2 = swap(x2, "fsdp", 2, line)
    x1 = swap(x1, "fsdp", 1, line)
    img = note(
        whole(
            image_kernel,
            jax.ShapeDtypeStruct((3, deep), F32),
            w_query,
            w_key,
            w_value,
            after(u_query[None] + 0.0),
            u_key[None],
            u_value[None],
        )
    )
    img = note(img + swap(img, "tp", 1, tp_count))
    img = note(img + swap(img, "tp", 2, tp_count))
    back = note(
        whole(
            back_kernel,
            jax.ShapeDtypeStruct((1, total + 128), F32),
            w_query,
            w_key,
            w_value,
            img,
        )
    )
    back_x = swap(back, "rep", 1, reps)

    def joint(a, b):
        return note(jnp.concatenate([a, after(b)], axis=0))

    def joined(p, x):
        return note((p + after(x).astype(F32)).astype(HALF))

    x3e = arrived(x3e)
    y3e = swap_tp(x3e, 2, ends)
    rows0 = note(
        gather_blocks(
            after(where),
            (tokens,),
            (piece(tp_count * quarter, reps * deep),),
            slab(0, 0, 0, (0, 2, 1, 3)),
        )[0]
    )
    x2 = arrived(x2)
    y2 = swap_tp(x2, 2, everyone)
    x1 = arrived(x1)
    x3m = across(after(x3m))
    w = [(own_w[0], arrived(other_w[0])), None]
    back = note(back + after(back_x))
    other_w[1] = swap(after(own_w[1]), "rep", 1, reps)
    pair = joint(x3e, y3e)
    c3e = swap_tp(pair, 1, ends)
    back = note(back + after(swap(after(back), "fsdp", 1, line)))
    rows3e = joint(pair, c3e)
    a3 = [out(note(product(after(rows3e), w[0]).astype(HALF))), None]
    y1 = swap_tp(after(x1), 2, everyone)
    pair1 = joint(x1, y1)
    pair2 = joint(x2, y2)
    w[1] = (own_w[1], arrived(other_w[1]))
    a3[1] = out(note(product(after(rows3e), w[1]).astype(HALF)))
    a3[0] = arrived(a3[0])
    x3m = arrived(x3m)
    back_z = swap(after(back), "fsdp", 2, line)
    c2 = swap_tp(after(pair2), 1, everyone)
    c1 = swap_tp(after(pair1), 1, everyone)
    c3m = swap_tp(after(x3m), 1, mids)
    rows2 = joint(pair2, c2)
    p2 = [note(product(after(rows2), w[0])), None]
    v = joined(p2[0], a3[0])
    a2e, a2m = [out(v), None], [across(v), None]
    back = note(back + after(back_z))
    rows1 = joint(pair1, c1)
    rows3m = joint(x3m, c3m)
    p2[1] = note(product(after(rows2), w[1]))
    back, squares = note(whole(functools.partial(length_kernel, widths), (row, lanes), back))
    p3m = [note(product(after(rows3m), w[0])), None]
    a2m[0] = arrived(a2m[0])
    a2e[0] = arrived(a2e[0])
    v = joined(p2[1], a3[1])
    a2e[1], a2m[1] = out(v), across(v)
    a1m = [across(joined(p3m[0], a2e[0])), None]
    p1 = [note(product(after(rows1), w[0])), None]
    a1p = [swap(joined(p1[0], a2m[0]), "fsdp", 1, line), None]
    squares = note(squares + after(swap(after(squares), "tp", 1, tp_count)))
    squares = note(squares + after(swap(squares, "tp", 2, tp_count)))
    a2m[1] = arrived(a2m[1])
    a2e[1] = arrived(a2e[1])
    p1[1] = note(product(after(rows1), w[1]))
    a1p[1] = swap(joined(p1[1], a2m[1]), "fsdp", 1, line)
    p3m[1] = note(product(after(rows3m), w[1]))
    a1m[1] = across(joined(p3m[1], a2e[1]))
    p0 = [note(product(after(rows0), w[c])) for c in range(2)]
    states = note(
        whole(
            functools.partial(state_kernel, widths, tp_count),
            tuple(jax.ShapeDtypeStruct((1, n), F32) for n in widths) + (lanes, row),
            back,
            after(squares),
            gammas,
        )
    )
    factors = states[4]
    factor = [factors[:, :wide], factors[:, wide:]]

    def packed(c):
        near, far = after((a1p[c], a1m[c]))
        return note((factor[c] * (p0[c] + near.astype(F32) + far.astype(F32))).astype(BF16))

    first = packed(0)
    ctx, keys, values = note(context_call(where, order.token, first, q_width))
    second = packed(1)
    context = context_call(where, order.token, second, q_width, (keys, values), ctx)
    return (context, states[0][0], states[1][0], states[2][0], states[3][0, :3])


def solution(mesh):
    in_specs = (
        P(("rep", "fsdp"), None),
        P(("rep", "fsdp"), None),
        P(("rep", "fsdp"), "tp"),
        P(("rep", "fsdp"), "tp"),
        P(("rep", "fsdp"), "tp"),
        P("tp"),
        P("tp"),
        P("tp"),
        P(),
    )
    out_specs = (P(("rep", "fsdp"), "tp"), P("tp"), P("tp"), P("tp"), P())
    sizes = tuple(mesh.shape[name] for name in ("rep", "fsdp", "tp"))
    body = line_body if sizes == (2, 4, 4) else gather_body
    return jax.shard_map(body, mesh=mesh, in_specs=in_specs, out_specs=out_specs, check_vma=False)
```
